32 devices in a mesh: groups: 2 (over y), ctx: 4 (over z), chan: 2 (over x), sub: 2 (over core).
Axes of the slice: x: 2, y: 2, z: 4, core: 2. Of those that a mesh axis runs over, the one named last changes fastest.
Arguments:
- sequence: bfloat16 [2048, 4096], P(('groups', 'ctx'), ('chan', 'sub')), parts along dimension 0, may hold values from -6 to 6
- gate: bfloat16 [2048, 4096], P(('groups', 'ctx'), ('chan', 'sub')), parts along dimension 0, may hold values from -6 to 6
- filters: float32 [32, 768], P(('chan', 'sub')), may hold values from -0.21875 to 0.21875
- lengths: int32 [32], P(('chan', 'sub')), may hold values from 1 to 3, as said below
- gain: float32 [4096], P(('chan', 'sub')), may hold values from 0.5 to 2
- permutation: int32 [128], replicated, may hold values from 0 to 127, each once
Outputs:
- mixed: bfloat16 [2048, 4096], P(('groups', 'ctx'), ('chan', 'sub')), parts along dimension 0
The draws below stay inside these ranges and needn't reach their ends.
There are 2 independent parts, one for each index of `groups`. The reference program is written for one: setup_inputs(seed, part) draws one part's arguments, and reference() takes and returns one part's arrays. A program takes and returns all parts, laid end to end along the dimension named above; an argument that names none is the same for every part. Nothing has to cross between parts.
Inputs may be any that keep to these rules, and one draw needn't show every extreme that they name: Filter lengths in blocks of 256 taps; some group has length 3 and some group length 1. A permutation of the 128 channel indices of a group, the same for every group.
All inputs are finite; a program needn't handle non-finite values.
Results may differ from the reference program's by a relative error of at most 0.0065.
Values may be sent and summed in bfloat16 or wider, within the bound.
No kernel may reach another device: no remote copies, remote signals or barrier semaphores. Data moves between devices by JAX's collectives and lax.ppermute only.
A program may use at most 64 MiB of HBM per device.

```python
import math
import jax
import jax.numpy as jnp
from jax import lax

D = 4096
GW = 128
LMAX = 3
ROWS = 256
SEQ = 1024
G = 32
TAPS = 768


def draw_lengths(key, part):
    first, second, third = jax.random.split(key, 3)
    values = jax.random.randint(first, (G,), 1, LMAX + 1)
    longest = jax.random.randint(second, (), 0, G)
    values = values.at[longest].set(LMAX)
    shortest = (longest + 1 + jax.random.randint(third, (), 0, G - 1)) % G
    return values.at[shortest].set(1).astype(jnp.int32)


def levels(own_key, dims, pieces, low, largest):
    loudness, own = 1.0, jax.random.fold_in(own_key, 6)
    for dim, blocks in pieces:
        steps = jnp.exp(jax.random.uniform(jax.random.fold_in(own, dim), (blocks,), jnp.float32, low / len(pieces), largest / len(pieces)))
        loudness = loudness * jnp.repeat(steps, dims[dim] // blocks).reshape([-1 if axis == dim else 1 for axis in range(len(dims))])
    return loudness


def noise(key, extent, scale, limit, shards=(), held_as=jnp.bfloat16):
    values = jax.random.normal(key, extent, jnp.float32) * scale
    if len(shards) > 0:
        values = levels(key, extent, shards, -0.22, 0.18) * values
    return jnp.clip(values, min=-limit, max=limit).astype(held_as)


def setup_inputs(seed: int = 0, part: int = 0) -> dict:
    key_list = jax.random.split(jax.random.key(seed), 7)
    part_splits = jax.random.split(jax.random.fold_in(key_list[6], part), 7)
    return {
        "sequence": noise(part_splits[0], (SEQ, D), 1.0, 6.0, ((0, 4), (1, 4))),
        "gate": noise(part_splits[1], (SEQ, D), 1.0, 6.0, ((0, 4), (1, 4))),
        "filters": noise(key_list[2], (G, TAPS), TAPS ** -0.5, 0.21875, ((0, 4),), jnp.float32),
        "lengths": draw_lengths(jax.random.fold_in(key_list[6], 71), part),
        "gain": jnp.clip(jnp.exp(math.log(2.0) - 1.3862944 * jax.random.uniform(key_list[4], (D,), jnp.float32) ** levels(key_list[4], (D,), ((0, 4),), -0.2, 0.2)), 0.5, 2.0),
        "permutation": jax.random.permutation(key_list[5], GW).astype(jnp.int32),
    }


def rounded(values):
    return lax.optimization_barrier(values.astype(jnp.bfloat16)).astype(jnp.float32)


def causal(values, kernel):
    length = SEQ + TAPS

    def single(pair):
        column, taps_row = pair
        freq_v = jnp.fft.rfft(column, length, axis=0)
        freq_k = jnp.fft.rfft(taps_row, length)
        return jnp.fft.irfft(freq_v * freq_k[:, None], length, axis=0)[:SEQ]

    result = lax.map(single, (jnp.transpose(values, (1, 0, 2)), kernel))
    return jnp.transpose(result, (1, 0, 2)).astype(jnp.float32)


def reference(sequence, gate, filters, lengths, gain, permutation):
    tap_ids = jnp.arange(TAPS, dtype=jnp.int32)
    kernel = rounded(jnp.where(tap_ids[None, :] < lengths[:, None] * ROWS, filters, jnp.float32(0.0)))
    seq3 = sequence.astype(jnp.float32).reshape(SEQ, G, GW)
    gain3 = gain.reshape(G, GW)
    gated = rounded(seq3 * gain3[None])
    ahead = causal(gated, kernel)
    match = permutation[:, None] == jnp.arange(GW, dtype=jnp.int32)[None, :]
    gain_rc = jnp.sum(jnp.where(match[None], gain3[:, :, None], jnp.float32(0.0)), axis=1)
    flipped = rounded(seq3 * gain_rc[None])
    behind = rounded(causal(flipped[::-1], kernel)[::-1])
    mixed = gate.astype(jnp.float32).reshape(SEQ, G, GW) * (ahead + behind)
    return mixed.astype(jnp.bfloat16).reshape(SEQ, D)
```

```python
import functools

import jax
import jax.numpy as jnp
from jax import lax
from jax.experimental import pallas as pl
from jax.experimental.pallas import tpu as pltpu
from jax.sharding import PartitionSpec as P

F32, BF16 = jnp.float32, jnp.bfloat16
VMEM, SMEM = pltpu.VMEM, pltpu.SMEM


def shifted(array, by):
    count = lax.axis_size("ctx")
    return lax.ppermute(array, "ctx", [(i, i + by) for i in range(count) if 0 <= i + by < count])


def rotated(array, by):
    count = lax.axis_size("ctx")
    return lax.ppermute(array, "ctx", [(i, (i + by) % count) for i in range(count)])


def held(array):
    return pltpu.with_memory_space_constraint(array, VMEM)


def build_kernel(rows, lags, owned, filters_ref, lengths_ref, gain_ref, perm_ref, fwd_ref, bwd_ref, gains_ref):
    first = lax.axis_index("ctx") * owned
    group_w = perm_ref.shape[1]
    taps = filters_ref.shape[1]
    span = lags * rows
    target = lax.broadcasted_iota(jnp.int32, (group_w, group_w), 0)
    match = perm_ref[...] == target
    for own in range(owned):
        group = first + own
        taps_row = filters_ref[pl.ds(group, 1), :]
        tap_ids = lax.broadcasted_iota(jnp.int32, (1, taps), 1)
        taps_row = jnp.where(tap_ids < lengths_ref[group] * rows, taps_row, 0.0)
        taps_row = jnp.concatenate([taps_row, jnp.zeros((1, span - taps), F32)], axis=1)
        strip = pltpu.roll(jnp.broadcast_to(taps_row, (rows, span)), 0, 1, stride=1, stride_axis=0)
        for lag in range(lags):
            block = strip[:, lag * rows : (lag + 1) * rows]
            bwd_ref[own, lag] = block.astype(BF16)
            fwd_ref[own, lag] = block.T.astype(BF16)
        gain_row = gain_ref[pl.ds(group, 1), :]
        spread = jnp.where(match, gain_row, 0.0)
        gains_ref[own, 0:1, :] = gain_row
        gains_ref[own, 1:2, :] = jnp.sum(spread.T, axis=0, keepdims=True)


def mix_kernel(count, lags, owned, *refs):
    blocks, (fwd_ref, bwd_ref, gains_ref) = refs[:count], refs[count : count + 3]
    outs, (inputs, sums) = refs[count + 3 : 2 * count + 3], refs[2 * count + 3 :]
    me = lax.axis_index("ctx")
    group_w = gains_ref.shape[2]
    places = [lax.rem(me - k + count, count) for k in range(count)]
    for k in range(count):
        inputs[places[k]] = blocks[k][...]
    for own in range(owned):
        lanes = slice(own * group_w, (own + 1) * group_w)
        values = jnp.concatenate([inputs[i, :, lanes] for i in range(count)], axis=1).astype(F32)
        gated = (values * jnp.tile(gains_ref[own, 0:1, :], (1, count))).astype(BF16)
        flipped = (values * jnp.tile(gains_ref[own, 1:2, :], (1, count))).astype(BF16)
        ahead = [None] * count
        behind = [None] * count

        def add(total, at, value):
            total[at] = value if total[at] is None else total[at] + value

        for lag in range(min(lags, count)):
            kept = (count - lag) * group_w
            up = jnp.dot(fwd_ref[own, lag], gated[:, :kept], preferred_element_type=F32)
            down = jnp.dot(bwd_ref[own, lag], flipped[:, count * group_w - kept :], preferred_element_type=F32)
            for i in range(count - lag):
                piece = slice(i * group_w, (i + 1) * group_w)
                add(ahead, i + lag, up[:, piece])
                add(behind, i, down[:, piece])
        for i in range(count):
            sums[i, :, lanes] = (ahead[i] + behind[i].astype(BF16).astype(F32)).astype(BF16)
    for k in range(count):
        outs[k][...] = sums[places[k]]


def gate_kernel(count, gate_ref, *refs):
    blocks, out_ref = refs[:count], refs[count]
    me = lax.axis_index("ctx")
    width = blocks[0].shape[1]
    for k in range(count):
        place = pl.ds(pl.multiple_of(lax.rem(me + k, count) * width, width), width)
        out_ref[:, place] = (gate_ref[:, place].astype(F32) * blocks[k][...].astype(F32)).astype(BF16)


def dealt(sequence, gate, filters, lengths, gain, permutation):
    rows, width = sequence.shape
    count = lax.axis_size("ctx")
    groups_dev, taps = filters.shape
    group_w = permutation.shape[0]
    owned = groups_dev // count
    lags = taps // rows + 1
    chunk = owned * group_w
    me = lax.axis_index("ctx")
    vmem = pl.BlockSpec(memory_space=VMEM)

    def part(k):
        return lax.dynamic_slice(sequence, (0, lax.rem(me + k, count) * chunk), (rows, chunk))

    blocks = [part(0)] + [rotated(part(k), k) for k in range(1, count)]
    fwd, bwd, gains = pl.pallas_call(
        functools.partial(build_kernel, rows, lags, owned),
        in_specs=[vmem, pl.BlockSpec(memory_space=SMEM), vmem, vmem],
        out_specs=[vmem] * 3,
        out_shape=[VMEM((owned, lags, rows, rows), BF16)] * 2 + [VMEM((owned, 8, group_w), F32)],
        name="build",
    )(filters, lengths, gain.reshape(groups_dev, group_w), permutation.reshape(1, group_w))
    outs = pl.pallas_call(
        functools.partial(mix_kernel, count, lags, owned),
        in_specs=[vmem] * (count + 3),
        out_specs=[vmem] * count,
        out_shape=[VMEM((rows, chunk), BF16)] * count,
        scratch_shapes=[VMEM((count, rows, chunk), BF16)] * 2,
        name="mix",
    )(*map(held, [*blocks, fwd, bwd, gains]))
    back = [outs[0]] + [rotated(outs[k], -k) for k in range(1, count)]
    return pl.pallas_call(
        functools.partial(gate_kernel, count),
        in_specs=[vmem] * (count + 1),
        out_specs=vmem,
        out_shape=jax.ShapeDtypeStruct((rows, width), BF16),
        name="gate",
    )(gate, *map(held, back))


def build_blocks(kernel, rows):
    groups_dev, taps = kernel.shape
    padded = jnp.pad(kernel, ((0, 0), (rows, rows)))
    blocks = []
    for lag in range(taps // rows + 1):
        window = padded[:, lag * rows : lag * rows + 2 * rows][:, ::-1]
        tiled = jnp.tile(window, (1, rows))[:, : rows * (2 * rows - 1)]
        skewed = tiled.reshape(groups_dev, rows, 2 * rows - 1)
        blocks.append(skewed[:, :, rows - 1 : 2 * rows - 1])
    return blocks


def halos(sequence, gate, filters, lengths, gain, permutation):
    rows, width = sequence.shape
    groups_dev = filters.shape[0]
    group_w = permutation.shape[0]
    tap_ids = lax.broadcasted_iota(jnp.int32, filters.shape, 1)
    kernel = jnp.where(tap_ids < lengths[:, None] * rows, filters, 0.0).astype(BF16)
    blocks = build_blocks(kernel, rows)
    gain3 = gain.reshape(groups_dev, group_w)
    target_ids = lax.broadcasted_iota(jnp.int32, (group_w, group_w), 1)
    match = permutation[:, None] == target_ids
    gain_rc = jnp.sum(jnp.where(match[None], gain3[:, :, None], 0.0), axis=1)

    def scaled(block, gains):
        return (block.reshape(rows, groups_dev, group_w).astype(F32) * gains[None]).astype(BF16)

    ahead, behind = 0.0, 0.0
    for lag, matrix in enumerate(blocks):
        past = scaled(shifted(sequence, lag) if lag else sequence, gain3)
        later = scaled(shifted(sequence, -lag) if lag else sequence, gain_rc)
        ahead = ahead + jnp.einsum("gst,tgc->sgc", matrix, past, preferred_element_type=F32)
        behind = behind + jnp.einsum("gts,tgc->sgc", matrix, later, preferred_element_type=F32)
    gate3 = gate.reshape(rows, groups_dev, group_w).astype(F32)
    mixed = gate3 * (ahead + behind.astype(BF16).astype(F32))
    return mixed.astype(BF16).reshape(rows, width)


def body(*args):
    count = lax.axis_size("ctx")
    groups_dev = args[2].shape[0]
    if count <= 8 and groups_dev % count == 0:
        return dealt(*args)
    return halos(*args)


def solution(mesh):
    in_specs = (
        P(("groups", "ctx"), ("chan", "sub")),
        P(("groups", "ctx"), ("chan", "sub")),
        P(("chan", "sub"), None),
        P(("chan", "sub")),
        P(("chan", "sub")),
        P(),
    )
    out_specs = P(("groups", "ctx"), ("chan", "sub"))
    return jax.shard_map(body, mesh=mesh, in_specs=in_specs, out_specs=out_specs, check_vma=False)
```

```python
import functools

import jax
import jax.numpy as jnp
from jax import lax
from jax.experimental import pallas as pl
from jax.experimental.pallas import tpu as pltpu
from jax.sharding import PartitionSpec as P

F32, BF16 = jnp.float32, jnp.bfloat16
VMEM, SMEM = pltpu.VMEM, pltpu.SMEM


def shifted(array, by):
    count = lax.axis_size("ctx")
    return lax.ppermute(array, "ctx", [(i, i + by) for i in range(count) if 0 <= i + by < count])


def rotated(array, by):
    count = lax.axis_size("ctx")
    return lax.ppermute(array, "ctx", [(i, (i + by) % count) for i in range(count)])


def held(array):
    return pltpu.with_memory_space_constraint(array, VMEM)


def build_kernel(rows, lags, owned, filters_ref, lengths_ref, gain_ref, perm_ref, fwd_ref, bwd_ref, gains_ref):
    first = lax.axis_index("ctx") * owned
    group_w = perm_ref.shape[1]
    taps = filters_ref.shape[1]
    span = lags * rows
    target = lax.broadcasted_iota(jnp.int32, (group_w, group_w), 0)
    match = perm_ref[...] == target
    for own in range(owned):
        group = first + own
        taps_row = filters_ref[pl.ds(group, 1), :]
        tap_ids = lax.broadcasted_iota(jnp.int32, (1, taps), 1)
        taps_row = jnp.where(tap_ids < lengths_ref[group] * rows, taps_row, 0.0)
        taps_row = jnp.concatenate([taps_row, jnp.zeros((1, span - taps), F32)], axis=1)
        strip = pltpu.roll(jnp.broadcast_to(taps_row, (rows, span)), 0, 1, stride=1, stride_axis=0)
        for lag in range(lags):
            block = strip[:, lag * rows : (lag + 1) * rows]
            bwd_ref[own, lag] = block.astype(BF16)
            fwd_ref[own, lag] = block.T.astype(BF16)
        gain_row = gain_ref[pl.ds(group, 1), :]
        spread = jnp.where(match, gain_row, 0.0)
        gains_ref[own, 0:1, :] = gain_row
        gains_ref[own, 1:2, :] = jnp.sum(spread.T, axis=0, keepdims=True)


def mix_kernel(count, lags, own, *refs):
    blocks, (fwd_ref, bwd_ref, gains_ref) = refs[:count], refs[count : count + 3]
    outs, (inputs, sums) = refs[count + 3 : 2 * count + 3], refs[2 * count + 3 :]
    me = lax.axis_index("ctx")
    group_w = gains_ref.shape[2]
    places = [lax.rem(me - k + count, count) for k in range(count)]
    for k in range(count):
        inputs[places[k]] = blocks[k][...]
    values = jnp.concatenate([inputs[i] for i in range(count)], axis=1).astype(F32)
    gated = (values * jnp.tile(gains_ref[own, 0:1, :], (1, count))).astype(BF16)
    flipped = (values * jnp.tile(gains_ref[own, 1:2, :], (1, count))).astype(BF16)
    ahead = [None] * count
    behind = [None] * count

    def add(total, at, value):
        total[at] = value if total[at] is None else total[at] + value

    for lag in range(min(lags, count)):
        kept = (count - lag) * group_w
        up = jnp.dot(fwd_ref[own, lag], gated[:, :kept], preferred_element_type=F32)
        down = jnp.dot(bwd_ref[own, lag], flipped[:, count * group_w - kept :], preferred_element_type=F32)
        for i in range(count - lag):
            piece = slice(i * group_w, (i + 1) * group_w)
            add(ahead, i + lag, up[:, piece])
            add(behind, i, down[:, piece])
    for i in range(count):
        sums[i] = (ahead[i] + behind[i].astype(BF16).astype(F32)).astype(BF16)
    for k in range(count):
        outs[k][...] = sums[places[k]]


def gate_kernel(count, owned, own, gate_ref, *refs):
    blocks, out_ref, (pieces, sems) = refs[:count], refs[-3], refs[-2:]
    me = lax.axis_index("ctx")
    group_w = blocks[0].shape[1]
    copies = []
    for k in range(count):
        at = (lax.rem(me + k, count) * owned + own) * group_w
        place = pl.ds(pl.multiple_of(at, group_w), group_w)
        pieces[k] = (gate_ref[:, place].astype(F32) * blocks[k][...].astype(F32)).astype(BF16)
        copies.append(pltpu.make_async_copy(pieces.at[k], out_ref.at[:, place], sems.at[k]))
        copies[k].start()
    for copy in copies:
        copy.wait()


def dealt(sequence, gate, filters, lengths, gain, permutation):
    rows, width = sequence.shape
    count = lax.axis_size("ctx")
    groups_dev, taps = filters.shape
    group_w = permutation.shape[0]
    owned = groups_dev // count
    lags = taps // rows + 1
    me = lax.axis_index("ctx")
    vmem, anywhere = pl.BlockSpec(memory_space=VMEM), pl.BlockSpec(memory_space=pl.ANY)

    def part(k, own):
        group = lax.rem(me + k, count) * owned + own
        return lax.dynamic_slice(sequence, (0, group * group_w), (rows, group_w))

    def deal(own):
        return [part(0, own)] + [rotated(part(k, own), k) for k in range(1, count)]

    blocks = [deal(own) for own in range(owned)]
    toeplitz = pl.pallas_call(
        functools.partial(build_kernel, rows, lags, owned),
        in_specs=[vmem, pl.BlockSpec(memory_space=SMEM), vmem, vmem],
        out_specs=[vmem] * 3,
        out_shape=[VMEM((owned, lags, rows, rows), BF16)] * 2 + [VMEM((owned, 8, group_w), F32)],
        name="build",
    )(filters, lengths, gain.reshape(groups_dev, group_w), permutation.reshape(1, group_w))
    back = []
    for own in range(owned):
        outs = pl.pallas_call(
            functools.partial(mix_kernel, count, lags, own),
            in_specs=[vmem] * (count + 3),
            out_specs=[vmem] * count,
            out_shape=[VMEM((rows, group_w), BF16)] * count,
            scratch_shapes=[VMEM((count, rows, group_w), BF16)] * 2,
            name=f"mix{own}",
        )(*map(held, [*blocks[own], *toeplitz]))
        back.append([outs[0]] + [rotated(outs[k], -k) for k in range(1, count)])
    gate = held(gate)
    out = []
    for own in range(owned):
        out = [
            pl.pallas_call(
                functools.partial(gate_kernel, count, owned, own),
                in_specs=[vmem] * (count + 1) + [anywhere] * len(out),
                out_specs=anywhere,
                out_shape=jax.ShapeDtypeStruct((rows, width), BF16),
                scratch_shapes=[VMEM((count, rows, group_w), BF16), pltpu.SemaphoreType.DMA((count,))],
                input_output_aliases={count + 1: 0} if out else {},
                name=f"gate{own}",
            )(gate, *map(held, back[own]), *out)
        ]
    return out[0]


def build_blocks(kernel, rows):
    groups_dev, taps = kernel.shape
    padded = jnp.pad(kernel, ((0, 0), (rows, rows)))
    blocks = []
    for lag in range(taps // rows + 1):
        window = padded[:, lag * rows : lag * rows + 2 * rows][:, ::-1]
        tiled = jnp.tile(window, (1, rows))[:, : rows * (2 * rows - 1)]
        skewed = tiled.reshape(groups_dev, rows, 2 * rows - 1)
        blocks.append(skewed[:, :, rows - 1 : 2 * rows - 1])
    return blocks


def halos(sequence, gate, filters, lengths, gain, permutation):
    rows, width = sequence.shape
    groups_dev = filters.shape[0]
    group_w = permutation.shape[0]
    tap_ids = lax.broadcasted_iota(jnp.int32, filters.shape, 1)
    kernel = jnp.where(tap_ids < lengths[:, None] * rows, filters, 0.0).astype(BF16)
    blocks = build_blocks(kernel, rows)
    gain3 = gain.reshape(groups_dev, group_w)
    target_ids = lax.broadcasted_iota(jnp.int32, (group_w, group_w), 1)
    match = permutation[:, None] == target_ids
    gain_rc = jnp.sum(jnp.where(match[None], gain3[:, :, None], 0.0), axis=1)

    def scaled(block, gains):
        return (block.reshape(rows, groups_dev, group_w).astype(F32) * gains[None]).astype(BF16)

    ahead, behind = 0.0, 0.0
    for lag, matrix in enumerate(blocks):
        past = scaled(shifted(sequence, lag) if lag else sequence, gain3)
        later = scaled(shifted(sequence, -lag) if lag else sequence, gain_rc)
        ahead = ahead + jnp.einsum("gst,tgc->sgc", matrix, past, preferred_element_type=F32)
        behind = behind + jnp.einsum("gts,tgc->sgc", matrix, later, preferred_element_type=F32)
    gate3 = gate.reshape(rows, groups_dev, group_w).astype(F32)
    mixed = gate3 * (ahead + behind.astype(BF16).astype(F32))
    return mixed.astype(BF16).reshape(rows, width)


def body(*args):
    count = lax.axis_size("ctx")
    groups_dev = args[2].shape[0]
    if count <= 8 and groups_dev % count == 0:
        return dealt(*args)
    return halos(*args)


def solution(mesh):
    in_specs = (
        P(("groups", "ctx"), ("chan", "sub")),
        P(("groups", "ctx"), ("chan", "sub")),
        P(("chan", "sub"), None),
        P(("chan", "sub")),
        P(("chan", "sub")),
        P(),
    )
    out_specs = P(("groups", "ctx"), ("chan", "sub"))
    return jax.shard_map(body, mesh=mesh, in_specs=in_specs, out_specs=out_specs, check_vma=False)
```

```python
import functools

import jax
import jax.numpy as jnp
from jax import lax
from jax.experimental import pallas as pl
from jax.experimental.pallas import tpu as pltpu
from jax.sharding import PartitionSpec as P

F32, BF16 = jnp.float32, jnp.bfloat16
VMEM, SMEM = pltpu.VMEM, pltpu.SMEM


def shifted(array, by):
    count = lax.axis_size("ctx")
    return lax.ppermute(array, "ctx", [(i, i + by) for i in range(count) if 0 <= i + by < count])


def rotated(array, by):
    count = lax.axis_size("ctx")
    return lax.ppermute(array, "ctx", [(i, (i + by) % count) for i in range(count)])


def held(array):
    return pltpu.with_memory_space_constraint(array, VMEM)


def build_kernel(rows, lags, owned, filters_ref, lengths_ref, gain_ref, perm_ref, fwd_ref, bwd_ref, gains_ref):
    first = lax.axis_index("ctx") * owned
    group_w = perm_ref.shape[1]
    taps = filters_ref.shape[1]
    span = lags * rows
    target = lax.broadcasted_iota(jnp.int32, (group_w, group_w), 0)
    match = perm_ref[...] == target
    for own in range(owned):
        group = first + own
        taps_row = filters_ref[pl.ds(group, 1), :]
        tap_ids = lax.broadcasted_iota(jnp.int32, (1, taps), 1)
        taps_row = jnp.where(tap_ids < lengths_ref[group] * rows, taps_row, 0.0)
        taps_row = jnp.concatenate([taps_row, jnp.zeros((1, span - taps), F32)], axis=1)
        strip = pltpu.roll(jnp.broadcast_to(taps_row, (rows, span)), 0, 1, stride=1, stride_axis=0)
        for lag in range(lags):
            block = strip[:, lag * rows : (lag + 1) * rows]
            bwd_ref[own, lag] = block.astype(BF16)
            fwd_ref[own, lag] = block.T.astype(BF16)
        gain_row = gain_ref[pl.ds(group, 1), :]
        spread = jnp.where(match, gain_row, 0.0)
        gains_ref[own, 0:1, :] = gain_row
        gains_ref[own, 1:2, :] = jnp.sum(spread.T, axis=0, keepdims=True)


def deal_kernel(count, chunks, group_w, owned, x_ref, *refs):
    outs, sems = refs[:-1], refs[-1]
    me = lax.axis_index("ctx")
    copies = []
    for c, chunk in enumerate(chunks):
        for k in range(count):
            at = (lax.rem(me + k, count) * owned + chunk[0]) * group_w
            place = pl.ds(pl.multiple_of(at, group_w), len(chunk) * group_w)
            copies.append(pltpu.make_async_copy(x_ref.at[:, place], outs[c * count + k], sems.at[c * count + k]))
            copies[-1].start()
    for copy in copies:
        copy.wait()


def mix_kernel(count, lags, chunk, order, *refs):
    blocks, (fwd_ref, bwd_ref, gains_ref) = dict(zip(order, refs[:count])), refs[count : count + 3]
    outs, (inputs, sums) = refs[count + 3 : 2 * count + 3], refs[2 * count + 3 :]
    me = lax.axis_index("ctx")
    group_w = gains_ref.shape[2]
    places = [lax.rem(me - k + count, count) for k in range(count)]
    for k in range(count):
        inputs[places[k]] = blocks[k][...]
    for j, own in enumerate(chunk):
        lanes = slice(j * group_w, (j + 1) * group_w)
        values = jnp.concatenate([inputs[i, :, lanes] for i in range(count)], axis=1).astype(F32)
        gated = (values * jnp.tile(gains_ref[own, 0:1, :], (1, count))).astype(BF16)
        flipped = (values * jnp.tile(gains_ref[own, 1:2, :], (1, count))).astype(BF16)
        ahead = [None] * count
        behind = [None] * count

        def add(total, at, value):
            total[at] = value if total[at] is None else total[at] + value

        for lag in range(min(lags, count)):
            kept = (count - lag) * group_w
            up = jnp.dot(fwd_ref[own, lag], gated[:, :kept], preferred_element_type=F32)
            down = jnp.dot(bwd_ref[own, lag], flipped[:, count * group_w - kept :], preferred_element_type=F32)
            for i in range(count - lag):
                piece = slice(i * group_w, (i + 1) * group_w)
                add(ahead, i + lag, up[:, piece])
                add(behind, i, down[:, piece])
        for i in range(count):
            sums[i, :, lanes] = (ahead[i] + behind[i].astype(BF16).astype(F32)).astype(BF16)
    for k in range(count):
        outs[k][...] = sums[places[k]]


def gate_kernel(count, owned, chunk, order, group_w, gate_ref, *refs):
    blocks, out_ref, (pieces, sems) = dict(zip(order, refs[:count])), refs[-3], refs[-2:]
    me = lax.axis_index("ctx")
    copies = []
    for k in range(count):
        at = (lax.rem(me + k, count) * owned + chunk[0]) * group_w
        place = pl.ds(pl.multiple_of(at, group_w), len(chunk) * group_w)
        pieces[k] = (gate_ref[:, place].astype(F32) * blocks[k][...].astype(F32)).astype(BF16)
        copies.append(pltpu.make_async_copy(pieces.at[k], out_ref.at[:, place], sems.at[k]))
        copies[k].start()
    for copy in copies:
        copy.wait()


def dealt(sequence, gate, filters, lengths, gain, permutation):
    rows, width = sequence.shape
    count = lax.axis_size("ctx")
    groups_dev, taps = filters.shape
    group_w = permutation.shape[0]
    owned = groups_dev // count
    lags = taps // rows + 1
    vmem, anywhere = pl.BlockSpec(memory_space=VMEM), pl.BlockSpec(memory_space=pl.ANY)
    params = pltpu.CompilerParams(vmem_limit_bytes=24 << 20)
    chunks = [(own,) for own in range(owned)]
    order = (0, 1, 2, 3)

    dealt_out = pl.pallas_call(
        functools.partial(deal_kernel, count, chunks, group_w, owned),
        in_specs=[anywhere],
        out_specs=[vmem] * (count * len(chunks)),
        out_shape=[VMEM((rows, len(chunk) * group_w), BF16) for chunk in chunks for _ in range(count)],
        scratch_shapes=[pltpu.SemaphoreType.DMA((count * len(chunks),))],
        compiler_params=params,
        name="deal",
    )(sequence)
    blocks = [
        [part if k == 0 else rotated(part, k) for k, part in enumerate(dealt_out[c * count : (c + 1) * count])]
        for c in range(len(chunks))
    ]
    toeplitz = pl.pallas_call(
        functools.partial(build_kernel, rows, lags, owned),
        in_specs=[vmem, pl.BlockSpec(memory_space=SMEM), vmem, vmem],
        out_specs=[vmem] * 3,
        out_shape=[VMEM((owned, lags, rows, rows), BF16)] * 2 + [VMEM((owned, 8, group_w), F32)],
        compiler_params=params,
        name="build",
    )(filters, lengths, gain.reshape(groups_dev, group_w), permutation.reshape(1, group_w))
    back = []
    for c, chunk in enumerate(chunks):
        chunk_w = len(chunk) * group_w
        outs = pl.pallas_call(
            functools.partial(mix_kernel, count, lags, chunk, order),
            in_specs=[vmem] * (count + 3),
            out_specs=[vmem] * count,
            out_shape=[VMEM((rows, chunk_w), BF16)] * count,
            scratch_shapes=[VMEM((count, rows, chunk_w), BF16)] * 2,
            compiler_params=params,
            name=f"mix{c}",
        )(*map(held, [*[blocks[c][k] for k in order], *toeplitz]))
        back.append([outs[0]] + [rotated(outs[k], -k) for k in range(1, count)])
    gate = held(gate)
    order = (0, 3, 2, 1)
    out = []
    for c, chunk in enumerate(chunks):
        out = [
            pl.pallas_call(
                functools.partial(gate_kernel, count, owned, chunk, order, group_w),
                in_specs=[vmem] * (count + 1) + [anywhere] * len(out),
                out_specs=anywhere,
                out_shape=jax.ShapeDtypeStruct((rows, width), BF16),
                scratch_shapes=[VMEM((count, rows, len(chunk) * group_w), BF16), pltpu.SemaphoreType.DMA((count,))],
                input_output_aliases={count + 1: 0} if out else {},
                compiler_params=params,
                name=f"gate{c}",
            )(gate, *map(held, [back[c][k] for k in order]), *out)
        ]
    return out[0]


def build_blocks(kernel, rows):
    groups_dev, taps = kernel.shape
    padded = jnp.pad(kernel, ((0, 0), (rows, rows)))
    blocks = []
    for lag in range(taps // rows + 1):
        window = padded[:, lag * rows : lag * rows + 2 * rows][:, ::-1]
        tiled = jnp.tile(window, (1, rows))[:, : rows * (2 * rows - 1)]
        skewed = tiled.reshape(groups_dev, rows, 2 * rows - 1)
        blocks.append(skewed[:, :, rows - 1 : 2 * rows - 1])
    return blocks


def halos(sequence, gate, filters, lengths, gain, permutation):
    rows, width = sequence.shape
    groups_dev = filters.shape[0]
    group_w = permutation.shape[0]
    tap_ids = lax.broadcasted_iota(jnp.int32, filters.shape, 1)
    kernel = jnp.where(tap_ids < lengths[:, None] * rows, filters, 0.0).astype(BF16)
    blocks = build_blocks(kernel, rows)
    gain3 = gain.reshape(groups_dev, group_w)
    target_ids = lax.broadcasted_iota(jnp.int32, (group_w, group_w), 1)
    match = permutation[:, None] == target_ids
    gain_rc = jnp.sum(jnp.where(match[None], gain3[:, :, None], 0.0), axis=1)

    def scaled(block, gains):
        return (block.reshape(rows, groups_dev, group_w).astype(F32) * gains[None]).astype(BF16)

    ahead, behind = 0.0, 0.0
    for lag, matrix in enumerate(blocks):
        past = scaled(shifted(sequence, lag) if lag else sequence, gain3)
        later = scaled(shifted(sequence, -lag) if lag else sequence, gain_rc)
        ahead = ahead + jnp.einsum("gst,tgc->sgc", matrix, past, preferred_element_type=F32)
        behind = behind + jnp.einsum("gts,tgc->sgc", matrix, later, preferred_element_type=F32)
    gate3 = gate.reshape(rows, groups_dev, group_w).astype(F32)
    mixed = gate3 * (ahead + behind.astype(BF16).astype(F32))
    return mixed.astype(BF16).reshape(rows, width)


def body(*args):
    count = lax.axis_size("ctx")
    groups_dev = args[2].shape[0]
    if count <= 8 and groups_dev % count == 0:
        return dealt(*args)
    return halos(*args)


def solution(mesh):
    in_specs = (
        P(("groups", "ctx"), ("chan", "sub")),
        P(("groups", "ctx"), ("chan", "sub")),
        P(("chan", "sub"), None),
        P(("chan", "sub")),
        P(("chan", "sub")),
        P(),
    )
    out_specs = P(("groups", "ctx"), ("chan", "sub"))
    return jax.shard_map(body, mesh=mesh, in_specs=in_specs, out_specs=out_specs, check_vma=False)
```

```python
import functools

import jax
import jax.numpy as jnp
from jax import lax
from jax.experimental import pallas as pl
from jax.experimental.pallas import tpu as pltpu
from jax.sharding import PartitionSpec as P

F32, BF16 = jnp.float32, jnp.bfloat16
VMEM, SMEM = pltpu.VMEM, pltpu.SMEM


def shifted(array, by):
    count = lax.axis_size("ctx")
    return lax.ppermute(array, "ctx", [(i, i + by) for i in range(count) if 0 <= i + by < count])


def rotated(array, by):
    count = lax.axis_size("ctx")
    return lax.ppermute(array, "ctx", [(i, (i + by) % count) for i in range(count)])


def held(array):
    return pltpu.with_memory_space_constraint(array, VMEM)


def build_kernel(rows, lags, owned, owns, filters_ref, lengths_ref, gain_ref, perm_ref, fwd_ref, bwd_ref, gains_ref):
    first = lax.axis_index("ctx") * owned
    group_w = perm_ref.shape[1]
    taps = filters_ref.shape[1]
    span = lags * rows
    target = lax.broadcasted_iota(jnp.int32, (group_w, group_w), 0)
    match = perm_ref[...] == target
    group_ids = lax.broadcasted_iota(jnp.int32, lengths_ref.shape, 1)
    tap_ids = lax.broadcasted_iota(jnp.int32, (1, taps), 1)
    for at, own in enumerate(owns):
        group = first + own
        length = jnp.sum(jnp.where(group_ids == group, lengths_ref[...], 0), axis=1, keepdims=True)
        taps_row = jnp.where(tap_ids < length * rows, filters_ref[pl.ds(group, 1), :], 0.0)
        taps_row = jnp.concatenate([taps_row, jnp.zeros((1, span - taps), F32)], axis=1)
        strip = pltpu.roll(jnp.broadcast_to(taps_row, (rows, span)), 0, 1, stride=1, stride_axis=0)
        for lag in range(lags):
            block = strip[:, lag * rows : (lag + 1) * rows]
            bwd_ref[at, lag] = block.astype(BF16)
            fwd_ref[at, lag] = block.T.astype(BF16)
        gain_row = gain_ref[pl.ds(group, 1), :]
        spread = jnp.where(match, gain_row, 0.0)
        gains_ref[at, 0:1, :] = gain_row
        gains_ref[at, 1:2, :] = jnp.sum(spread.T, axis=0, keepdims=True)


def deal_kernel(count, owned, group_w, messages, x_ref, *refs):
    sems = refs[-1]
    small = (len(refs) - 1 - len(messages)) // 2
    outs = refs[small:-1]
    me = lax.axis_index("ctx")
    copies = []
    for i, (k, chunk) in enumerate(messages):
        at = (lax.rem(me + k, count) * owned + chunk[0]) * group_w
        place = pl.ds(pl.multiple_of(at, group_w), len(chunk) * group_w)
        copies.append(pltpu.make_async_copy(x_ref.at[:, place], outs[i], sems.at[i]))
        copies[i].start()
    for i in range(small):
        at = len(messages) + i
        copies.append(pltpu.make_async_copy(refs[i], outs[at], sems.at[at]))
        copies[at].start()
    for copy in copies:
        copy.wait()


def mix_kernel(count, lags, own, messages, late, *refs):
    blocks, (fwd_ref, bwd_ref, gains_ref) = refs[:count], refs[count : count + 3]
    earlier, refs = refs[count + 3 : count + 3 + len(late)], refs[count + 3 + len(late) :]
    outs, (inputs, sums) = refs[:count], refs[count:]
    me = lax.axis_index("ctx")
    group_w = gains_ref.shape[2]
    places = [lax.rem(me - k + count, count) for k in range(count)]
    for block, (k, chunk) in zip(blocks, messages):
        first = chunk.index(own) * group_w
        inputs[places[k]] = block[:, first : first + group_w]
    values = jnp.concatenate([inputs[i] for i in range(count)], axis=1).astype(F32)
    gated = (values * jnp.tile(gains_ref[own, 0:1, :], (1, count))).astype(BF16)
    flipped = (values * jnp.tile(gains_ref[own, 1:2, :], (1, count))).astype(BF16)
    ahead = [None] * count
    behind = [None] * count

    def add(total, at, value):
        total[at] = value if total[at] is None else total[at] + value

    for lag in range(min(lags, count)):
        kept = (count - lag) * group_w
        up = jnp.dot(fwd_ref[own, lag], gated[:, :kept], preferred_element_type=F32)
        down = jnp.dot(bwd_ref[own, lag], flipped[:, count * group_w - kept :], preferred_element_type=F32)
        for i in range(count - lag):
            piece = slice(i * group_w, (i + 1) * group_w)
            add(ahead, i + lag, up[:, piece])
            add(behind, i, down[:, piece])
    for i in range(count):
        sums[i] = (ahead[i] + behind[i].astype(BF16).astype(F32)).astype(BF16)
    for k in range(count):
        outs[k][:, outs[k].shape[1] - group_w :] = sums[places[k]]
    for k, ref in zip(late, earlier):
        outs[k][:, :group_w] = ref[...]


def gate_kernel(count, owned, messages, group_w, gate_ref, *refs):
    blocks, out_ref, (pieces, sems) = refs[: len(messages)], refs[-3], refs[-2:]
    me = lax.axis_index("ctx")
    copies = []
    for i, (k, chunk) in enumerate(messages):
        at = (lax.rem(me + k, count) * owned + chunk[0]) * group_w
        place = pl.ds(pl.multiple_of(at, group_w), len(chunk) * group_w)
        mixed = (gate_ref[:, place].astype(F32) * blocks[i][...].astype(F32)).astype(BF16)
        piece = pieces.at[i, :, : len(chunk) * group_w]
        piece[...] = mixed
        copies.append(pltpu.make_async_copy(piece, out_ref.at[:, place], sems.at[i]))
        copies[i].start()
    for copy in copies:
        copy.wait()


def dealt(sequence, gate, filters, lengths, gain, permutation):
    rows, width = sequence.shape
    count = lax.axis_size("ctx")
    groups_dev, taps = filters.shape
    group_w = permutation.shape[0]
    owned = groups_dev // count
    lags = taps // rows + 1
    vmem, anywhere = pl.BlockSpec(memory_space=VMEM), pl.BlockSpec(memory_space=pl.ANY)
    params = pltpu.CompilerParams(vmem_limit_bytes=24 << 20)
    deals = (((2, (0,)), (1, (0,)), (3, (0,)), (2, (1,)), (1, (1,)), (3, (1,)), (0, (0,)), (0, (1,))),)
    used = (((0, (0,)), (2, (0,)), (1, (0,)), (3, (0,))), ((0, (1,)), (2, (1,)), (1, (1,)), (3, (1,))))
    gates = (((0, (0,)), (3, (0,)), (2, (0,)), (1, (0,))), ((0, (1,)), (3, (1,)), (2, (1,)), (1, (1,))))

    sequence = pltpu.with_memory_space_constraint(sequence, pltpu.HBM)
    sent = {}
    small = [
        filters,
        lengths.reshape(1, groups_dev),
        gain.reshape(groups_dev, group_w),
        permutation.reshape(1, group_w),
    ]
    small = [pltpu.with_memory_space_constraint(array, pltpu.HBM) for array in small]
    for d, messages in enumerate(deals):
        fetched = [] if d else small
        parts = pl.pallas_call(
            functools.partial(deal_kernel, count, owned, group_w, messages),
            in_specs=[anywhere] * (1 + len(fetched)),
            out_specs=[vmem] * (len(messages) + len(fetched)),
            out_shape=[VMEM((rows, len(chunk) * group_w), BF16) for _, chunk in messages]
            + [VMEM(array.shape, array.dtype) for array in fetched],
            scratch_shapes=[pltpu.SemaphoreType.DMA((len(messages) + len(fetched),))],
            compiler_params=params,
            name=f"deal{d}",
        )(sequence, *fetched)
        if fetched:
            small = parts[len(messages) :]
        for (k, chunk), part in zip(messages, parts):
            sent[k, chunk] = part if k == 0 else rotated(part, k)
    built = [
        pl.pallas_call(
            functools.partial(build_kernel, rows, lags, owned, owns),
            in_specs=[vmem] * 4,
            out_specs=[vmem] * 3,
            out_shape=[VMEM((len(owns), lags, rows, rows), BF16)] * 2 + [VMEM((len(owns), 8, group_w), F32)],
            compiler_params=params,
            name=f"build{owns[0]}",
        )(*map(held, small))
        for owns in [tuple(range(owned))]
    ]
    back = {}
    merged = ()
    for own in range(owned):
        late = merged if own else ()
        earlier = [outs[k] for k in late] if own else []
        outs = pl.pallas_call(
            functools.partial(mix_kernel, count, lags, own, used[own], late),
            in_specs=[vmem] * (count + 3 + len(late)),
            out_specs=[vmem] * count,
            out_shape=[VMEM((rows, 2 * group_w if k in late else group_w), BF16) for k in range(count)],
            scratch_shapes=[VMEM((count, rows, group_w), BF16)] * 2,
            compiler_params=params,
            name=f"mix{own}",
        )(*map(held, [*[sent[message] for message in used[own]], *built[0], *earlier]))
        for k in range(count):
            if k in merged and not own:
                continue
            chunk = (0, 1) if k in merged else (own,)
            back[k, chunk] = outs[k] if k == 0 else rotated(outs[k], -k)
    gate = held(gate)
    out = []
    for g, messages in enumerate(gates):
        widest = max(len(chunk) for _, chunk in messages) * group_w
        out = [
            pl.pallas_call(
                functools.partial(gate_kernel, count, owned, messages, group_w),
                in_specs=[vmem] * (len(messages) + 1) + [anywhere] * len(out),
                out_specs=anywhere,
                out_shape=jax.ShapeDtypeStruct((rows, width), BF16),
                scratch_shapes=[VMEM((len(messages), rows, widest), BF16), pltpu.SemaphoreType.DMA((len(messages),))],
                input_output_aliases={len(messages) + 1: 0} if out else {},
                compiler_params=params,
                name=f"gate{g}",
            )(gate, *[held(back[message]) for message in messages], *out)
        ]
    return out[0]


def build_blocks(kernel, rows):
    groups_dev, taps = kernel.shape
    padded = jnp.pad(kernel, ((0, 0), (rows, rows)))
    blocks = []
    for lag in range(taps // rows + 1):
        window = padded[:, lag * rows : lag * rows + 2 * rows][:, ::-1]
        tiled = jnp.tile(window, (1, rows))[:, : rows * (2 * rows - 1)]
        skewed = tiled.reshape(groups_dev, rows, 2 * rows - 1)
        blocks.append(skewed[:, :, rows - 1 : 2 * rows - 1])
    return blocks


def halos(sequence, gate, filters, lengths, gain, permutation):
    rows, width = sequence.shape
    groups_dev = filters.shape[0]
    group_w = permutation.shape[0]
    tap_ids = lax.broadcasted_iota(jnp.int32, filters.shape, 1)
    kernel = jnp.where(tap_ids < lengths[:, None] * rows, filters, 0.0).astype(BF16)
    blocks = build_blocks(kernel, rows)
    gain3 = gain.reshape(groups_dev, group_w)
    target_ids = lax.broadcasted_iota(jnp.int32, (group_w, group_w), 1)
    match = permutation[:, None] == target_ids
    gain_rc = jnp.sum(jnp.where(match[None], gain3[:, :, None], 0.0), axis=1)

    def scaled(block, gains):
        return (block.reshape(rows, groups_dev, group_w).astype(F32) * gains[None]).astype(BF16)

    ahead, behind = 0.0, 0.0
    for lag, matrix in enumerate(blocks):
        past = scaled(shifted(sequence, lag) if lag else sequence, gain3)
        later = scaled(shifted(sequence, -lag) if lag else sequence, gain_rc)
        ahead = ahead + jnp.einsum("gst,tgc->sgc", matrix, past, preferred_element_type=F32)
        behind = behind + jnp.einsum("gts,tgc->sgc", matrix, later, preferred_element_type=F32)
    gate3 = gate.reshape(rows, groups_dev, group_w).astype(F32)
    mixed = gate3 * (ahead + behind.astype(BF16).astype(F32))
    return mixed.astype(BF16).reshape(rows, width)


def body(*args):
    count = lax.axis_size("ctx")
    groups_dev = args[2].shape[0]
    if count == 4 and groups_dev == 2 * count:
        return dealt(*args)
    return halos(*args)


def solution(mesh):
    in_specs = (
        P(("groups", "ctx"), ("chan", "sub")),
        P(("groups", "ctx"), ("chan", "sub")),
        P(("chan", "sub"), None),
        P(("chan", "sub")),
        P(("chan", "sub")),
        P(),
    )
    out_specs = P(("groups", "ctx"), ("chan", "sub"))
    return jax.shard_map(body, mesh=mesh, in_specs=in_specs, out_specs=out_specs, check_vma=False)
```

```python
import functools

import jax
import jax.numpy as jnp
from jax import lax
from jax.experimental import pallas as pl
from jax.experimental.pallas import tpu as pltpu
from jax.sharding import PartitionSpec as P

F32, BF16 = jnp.float32, jnp.bfloat16
VMEM = pltpu.VMEM


def shifted(array, by):
    count = lax.axis_size("ctx")
    return lax.ppermute(array, "ctx", [(i, i + by) for i in range(count) if 0 <= i + by < count])


def rotated(array, by):
    count = lax.axis_size("ctx")
    return lax.ppermute(array, "ctx", [(i, (i + by) % count) for i in range(count)])


def held(array):
    return pltpu.with_memory_space_constraint(array, VMEM)


def rounds(count):
    if count == 4:
        return (2, 1, 3), (1, 2, 3)
    return (tuple(range(1, count)),) * 2


def lanes(by, own, count, owned, group_w):
    block = lax.rem(lax.axis_index("ctx") + by, count)
    return pl.ds(pl.multiple_of((block * owned + own) * group_w, group_w), group_w)


def build_kernel(rows, lags, owned, owns, filters_ref, lengths_ref, gain_ref, perm_ref, fwd_ref, bwd_ref, gains_ref):
    first = lax.axis_index("ctx") * owned
    group_w = perm_ref.shape[1]
    taps = filters_ref.shape[1]
    span = lags * rows
    target = lax.broadcasted_iota(jnp.int32, (group_w, group_w), 0)
    match = perm_ref[...] == target
    group_ids = lax.broadcasted_iota(jnp.int32, lengths_ref.shape, 1)
    tap_ids = lax.broadcasted_iota(jnp.int32, (1, taps), 1)
    for at, own in enumerate(owns):
        group = first + own
        length = jnp.sum(jnp.where(group_ids == group, lengths_ref[...], 0), axis=1, keepdims=True)
        taps_row = jnp.where(tap_ids < length * rows, filters_ref[pl.ds(group, 1), :], 0.0)
        taps_row = jnp.concatenate([taps_row, jnp.zeros((1, span - taps), F32)], axis=1)
        strip = pltpu.roll(jnp.broadcast_to(taps_row, (rows, span)), 0, 1, stride=1, stride_axis=0)
        for lag in range(lags):
            block = strip[:, lag * rows : (lag + 1) * rows]
            bwd_ref[at, lag] = block.astype(BF16)
            fwd_ref[at, lag] = block.T.astype(BF16)
        gain_row = gain_ref[pl.ds(group, 1), :]
        spread = jnp.where(match, gain_row, 0.0)
        gains_ref[at, 0:1, :] = gain_row
        gains_ref[at, 1:2, :] = jnp.sum(spread.T, axis=0, keepdims=True)


def deal_kernel(count, owned, group_w, messages, x_ref, *refs):
    sems = refs[-1]
    small = (len(refs) - 1 - len(messages)) // 2
    outs = refs[small:-1]
    sources = [x_ref.at[:, lanes(by, own, count, owned, group_w)] for own, by in messages] + list(refs[:small])
    copies = [pltpu.make_async_copy(source, outs[i], sems.at[i]) for i, source in enumerate(sources)]
    for copy in copies:
        copy.start()
    for copy in copies:
        copy.wait()


def mix_kernel(count, lags, own, out_order, back_order, *refs):
    blocks, (fwd_ref, bwd_ref, gains_ref) = refs[:count], refs[count : count + 3]
    outs, (inputs, sums) = refs[count + 3 : 2 * count + 3], refs[2 * count + 3 :]
    me = lax.axis_index("ctx")
    group_w = gains_ref.shape[2]
    for block, by in zip(blocks, (0, *out_order)):
        inputs[lax.rem(me - by + count, count)] = block[...]
    values = jnp.concatenate([inputs[i] for i in range(count)], axis=1).astype(F32)
    gated = (values * jnp.tile(gains_ref[own, 0:1, :], (1, count))).astype(BF16)
    flipped = (values * jnp.tile(gains_ref[own, 1:2, :], (1, count))).astype(BF16)
    ahead = [None] * count
    behind = [None] * count

    def add(total, at, value):
        total[at] = value if total[at] is None else total[at] + value

    for lag in range(min(lags, count)):
        kept = (count - lag) * group_w
        up = jnp.dot(fwd_ref[own, lag], gated[:, :kept], preferred_element_type=F32)
        down = jnp.dot(bwd_ref[own, lag], flipped[:, count * group_w - kept :], preferred_element_type=F32)
        for i in range(count - lag):
            piece = slice(i * group_w, (i + 1) * group_w)
            add(ahead, i + lag, up[:, piece])
            add(behind, i, down[:, piece])
    for i in range(count):
        sums[i] = (ahead[i] + behind[i].astype(BF16).astype(F32)).astype(BF16)
    for out, by in zip(outs, (0, *back_order)):
        out[...] = sums[lax.rem(me + by, count)]


def gate_kernel(count, owned, own, back_order, gate_ref, *refs):
    blocks, out_ref, (pieces, sems) = refs[:count], refs[-3], refs[-2:]
    group_w = blocks[0].shape[1]
    copies = []
    for i, by in enumerate((0, *back_order)):
        place = lanes(count - by, own, count, owned, group_w)
        pieces[i] = (gate_ref[:, place].astype(F32) * blocks[i][...].astype(F32)).astype(BF16)
        copies.append(pltpu.make_async_copy(pieces.at[i], out_ref.at[:, place], sems.at[i]))
        copies[i].start()
    for copy in copies:
        copy.wait()


def dealt(sequence, gate, filters, lengths, gain, permutation):
    rows, width = sequence.shape
    count = lax.axis_size("ctx")
    groups_dev, taps = filters.shape
    group_w = permutation.shape[0]
    owned = groups_dev // count
    lags = taps // rows + 1
    out_order, back_order = rounds(count)
    vmem, anywhere = pl.BlockSpec(memory_space=VMEM), pl.BlockSpec(memory_space=pl.ANY)
    params = pltpu.CompilerParams(vmem_limit_bytes=24 << 20)
    dma = pltpu.SemaphoreType.DMA

    small = [
        filters,
        lengths.reshape(1, groups_dev),
        gain.reshape(groups_dev, group_w),
        permutation.reshape(1, group_w),
    ]
    small = [pltpu.with_memory_space_constraint(array, pltpu.HBM) for array in small]
    messages = [(own, by) for own in range(owned) for by in out_order] + [(own, 0) for own in range(owned)]
    sent = {}
    for part, source, extra in (
        (messages[:1], pltpu.with_memory_space_constraint(sequence, pltpu.HBM), small),
        (messages[1:], sequence, []),
    ):
        copied = pl.pallas_call(
            functools.partial(deal_kernel, count, owned, group_w, part),
            in_specs=[anywhere] * (1 + len(extra)),
            out_specs=[vmem] * (len(part) + len(extra)),
            out_shape=[VMEM((rows, group_w), BF16) for _ in part] + [VMEM(array.shape, array.dtype) for array in extra],
            scratch_shapes=[dma((len(part) + len(extra),))],
            compiler_params=params,
            name="deal",
        )(source, *extra)
        sent.update({(own, by): rotated(array, by) if by else array for (own, by), array in zip(part, copied)})
        small = copied[len(part) :] if extra else small
    built = pl.pallas_call(
        functools.partial(build_kernel, rows, lags, owned, tuple(range(owned))),
        in_specs=[vmem] * 4,
        out_specs=[vmem] * 3,
        out_shape=[VMEM((owned, lags, rows, rows), BF16)] * 2 + [VMEM((owned, 8, group_w), F32)],
        compiler_params=params,
        name="build",
    )(*map(held, small))
    back = []
    for own in range(owned):
        outs = pl.pallas_call(
            functools.partial(mix_kernel, count, lags, own, out_order, back_order),
            in_specs=[vmem] * (count + 3),
            out_specs=[vmem] * count,
            out_shape=[VMEM((rows, group_w), BF16)] * count,
            scratch_shapes=[VMEM((count, rows, group_w), BF16)] * 2,
            compiler_params=params,
            name="mix",
        )(*map(held, [*[sent[own, by] for by in (0, *out_order)], *built]))
        back.append([rotated(array, by) if by else array for by, array in zip((0, *back_order), outs)])
    gate = held(gate)
    out = []
    for own in range(owned):
        out = [
            pl.pallas_call(
                functools.partial(gate_kernel, count, owned, own, back_order),
                in_specs=[vmem] * (count + 1) + [anywhere] * len(out),
                out_specs=anywhere,
                out_shape=jax.ShapeDtypeStruct((rows, width), BF16),
                scratch_shapes=[VMEM((count, rows, group_w), BF16), dma((count,))],
                input_output_aliases={count + 1: 0} if out else {},
                compiler_params=params,
                name="gate",
            )(gate, *map(held, back[own]), *out)
        ]
    return out[0]


def build_blocks(kernel, rows):
    groups_dev, taps = kernel.shape
    padded = jnp.pad(kernel, ((0, 0), (rows, rows)))
    blocks = []
    for lag in range(taps // rows + 1):
        window = padded[:, lag * rows : lag * rows + 2 * rows][:, ::-1]
        tiled = jnp.tile(window, (1, rows))[:, : rows * (2 * rows - 1)]
        skewed = tiled.reshape(groups_dev, rows, 2 * rows - 1)
        blocks.append(skewed[:, :, rows - 1 : 2 * rows - 1])
    return blocks


def halos(sequence, gate, filters, lengths, gain, permutation):
    rows, width = sequence.shape
    groups_dev = filters.shape[0]
    group_w = permutation.shape[0]
    tap_ids = lax.broadcasted_iota(jnp.int32, filters.shape, 1)
    kernel = jnp.where(tap_ids < lengths[:, None] * rows, filters, 0.0).astype(BF16)
    blocks = build_blocks(kernel, rows)
    gain3 = gain.reshape(groups_dev, group_w)
    target_ids = lax.broadcasted_iota(jnp.int32, (group_w, group_w), 1)
    match = permutation[:, None] == target_ids
    gain_rc = jnp.sum(jnp.where(match[None], gain3[:, :, None], 0.0), axis=1)

    def scaled(block, gains):
        return (block.reshape(rows, groups_dev, group_w).astype(F32) * gains[None]).astype(BF16)

    ahead, behind = 0.0, 0.0
    for lag, matrix in enumerate(blocks):
        past = scaled(shifted(sequence, lag) if lag else sequence, gain3)
        later = scaled(shifted(sequence, -lag) if lag else sequence, gain_rc)
        ahead = ahead + jnp.einsum("gst,tgc->sgc", matrix, past, preferred_element_type=F32)
        behind = behind + jnp.einsum("gts,tgc->sgc", matrix, later, preferred_element_type=F32)
    gate3 = gate.reshape(rows, groups_dev, group_w).astype(F32)
    mixed = gate3 * (ahead + behind.astype(BF16).astype(F32))
    return mixed.astype(BF16).reshape(rows, width)


def body(*args):
    count = lax.axis_size("ctx")
    groups_dev = args[2].shape[0]
    if count <= 8 and groups_dev % count == 0:
        return dealt(*args)
    return halos(*args)


def solution(mesh):
    in_specs = (
        P(("groups", "ctx"), ("chan", "sub")),
        P(("groups", "ctx"), ("chan", "sub")),
        P(("chan", "sub"), None),
        P(("chan", "sub")),
        P(("chan", "sub")),
        P(),
    )
    out_specs = P(("groups", "ctx"), ("chan", "sub"))
    return jax.shard_map(body, mesh=mesh, in_specs=in_specs, out_specs=out_specs, check_vma=False)
```

```python
import functools

import jax
import jax.numpy as jnp
from jax import lax
from jax.experimental import pallas as pl
from jax.experimental.pallas import tpu as pltpu
from jax.sharding import PartitionSpec as P

F32, BF16 = jnp.float32, jnp.bfloat16
VMEM = pltpu.VMEM


def shifted(array, by):
    count = lax.axis_size("ctx")
    return lax.ppermute(array, "ctx", [(i, i + by) for i in range(count) if 0 <= i + by < count])


def rotated(array, by):
    count = lax.axis_size("ctx")
    return lax.ppermute(array, "ctx", [(i, (i + by) % count) for i in range(count)])


def held(array):
    return pltpu.with_memory_space_constraint(array, VMEM)


def rounds(count):
    if count == 4:
        return (2, 1, 3), (1, 2, 3)
    return (tuple(range(1, count)),) * 2


def lanes(by, own, count, owned, group_w):
    block = lax.rem(lax.axis_index("ctx") + by, count)
    return pl.ds(pl.multiple_of((block * owned + own) * group_w, group_w), group_w)


def build_kernel(rows, lags, owned, owns, filters_ref, lengths_ref, gain_ref, perm_ref, fwd_ref, bwd_ref, gains_ref):
    first = lax.axis_index("ctx") * owned
    group_w = perm_ref.shape[1]
    taps = filters_ref.shape[1]
    span = lags * rows
    target = lax.broadcasted_iota(jnp.int32, (group_w, group_w), 0)
    match = perm_ref[...] == target
    group_ids = lax.broadcasted_iota(jnp.int32, lengths_ref.shape, 1)
    tap_ids = lax.broadcasted_iota(jnp.int32, (1, taps), 1)
    for at, own in enumerate(owns):
        group = first + own
        length = jnp.sum(jnp.where(group_ids == group, lengths_ref[...], 0), axis=1, keepdims=True)
        taps_row = jnp.where(tap_ids < length * rows, filters_ref[pl.ds(group, 1), :], 0.0)
        taps_row = jnp.concatenate([taps_row, jnp.zeros((1, span - taps), F32)], axis=1)
        strip = pltpu.roll(jnp.broadcast_to(taps_row, (rows, span)), 0, 1, stride=1, stride_axis=0)
        for lag in range(lags):
            block = strip[:, lag * rows : (lag + 1) * rows]
            bwd_ref[at, lag] = block.astype(BF16)
            fwd_ref[at, lag] = block.T.astype(BF16)
        gain_row = gain_ref[pl.ds(group, 1), :]
        spread = jnp.where(match, gain_row, 0.0)
        gains_ref[at, 0:1, :] = gain_row
        gains_ref[at, 1:2, :] = jnp.sum(spread.T, axis=0, keepdims=True)


def deal_kernel(count, owned, group_w, messages, x_ref, *refs):
    sems = refs[-1]
    small = (len(refs) - 1 - len(messages)) // 2
    outs = refs[small:-1]
    sources = [x_ref.at[:, lanes(by, own, count, owned, group_w)] for own, by in messages] + list(refs[:small])
    copies = [pltpu.make_async_copy(source, outs[i], sems.at[i]) for i, source in enumerate(sources)]
    for copy in copies:
        copy.start()
    for copy in copies:
        copy.wait()


def deal_build_kernel(count, rows, lags, owned, group_w, messages, x_ref, *refs):
    small, outs, built, sems = refs[:4], refs[4 : 4 + len(messages)], refs[4 + len(messages) : -1], refs[-1]
    copies = [
        pltpu.make_async_copy(x_ref.at[:, lanes(by, own, count, owned, group_w)], outs[i], sems.at[i])
        for i, (own, by) in enumerate(messages)
    ]
    for copy in copies:
        copy.start()
    build_kernel(rows, lags, owned, tuple(range(owned)), *small, *built)
    for copy in copies:
        copy.wait()


def mix_kernel(count, lags, own, out_order, back_order, *refs):
    for me in range(count):
        body = functools.partial(mix_at, me, count, lags, own, out_order, back_order, *refs)
        pl.when(lax.axis_index("ctx") == me)(body)


def mix_at(me, count, lags, own, out_order, back_order, *refs):
    blocks, (fwd_ref, bwd_ref, gains_ref), outs = refs[:count], refs[count : count + 3], refs[count + 3 :]
    group_w = gains_ref.shape[2]
    inputs = {(me - by) % count: block for block, by in zip(blocks, (0, *out_order))}
    sums = {(me + by) % count: out for out, by in zip(outs, (0, *back_order))}
    values = [inputs[i][...].astype(F32) for i in range(count)]
    gated = jnp.concatenate([(value * gains_ref[own, 0:1, :]).astype(BF16) for value in values], axis=1)
    flipped = jnp.concatenate([(value * gains_ref[own, 1:2, :]).astype(BF16) for value in values], axis=1)
    ahead = [None] * count
    behind = [None] * count

    def add(total, at, value):
        total[at] = value if total[at] is None else total[at] + value

    for lag in range(min(lags, count)):
        kept = (count - lag) * group_w
        up = jnp.dot(fwd_ref[own, lag], gated[:, :kept], preferred_element_type=F32)
        down = jnp.dot(bwd_ref[own, lag], flipped[:, count * group_w - kept :], preferred_element_type=F32)
        for i in range(count - lag):
            piece = slice(i * group_w, (i + 1) * group_w)
            add(ahead, i + lag, up[:, piece])
            add(behind, i, down[:, piece])
    for i in range(count):
        sums[i][...] = (ahead[i] + behind[i].astype(BF16).astype(F32)).astype(BF16)


def gate_kernel(count, owned, own, back_order, gate_ref, *refs):
    blocks, out_ref, (pieces, sems) = refs[:count], refs[-3], refs[-2:]
    group_w = blocks[0].shape[1]
    copies = []
    for i, by in enumerate((0, *back_order)):
        place = lanes(count - by, own, count, owned, group_w)
        pieces[i] = (gate_ref[:, place].astype(F32) * blocks[i][...].astype(F32)).astype(BF16)
        copies.append(pltpu.make_async_copy(pieces.at[i], out_ref.at[:, place], sems.at[i]))
        copies[i].start()
    for copy in copies:
        copy.wait()


def dealt(sequence, gate, filters, lengths, gain, permutation):
    rows, width = sequence.shape
    count = lax.axis_size("ctx")
    groups_dev, taps = filters.shape
    group_w = permutation.shape[0]
    owned = groups_dev // count
    lags = taps // rows + 1
    out_order, back_order = rounds(count)
    vmem, anywhere = pl.BlockSpec(memory_space=VMEM), pl.BlockSpec(memory_space=pl.ANY)
    params = pltpu.CompilerParams(vmem_limit_bytes=24 << 20)
    dma = pltpu.SemaphoreType.DMA

    small = [
        filters,
        lengths.reshape(1, groups_dev),
        gain.reshape(groups_dev, group_w),
        permutation.reshape(1, group_w),
    ]
    small = [pltpu.with_memory_space_constraint(array, pltpu.HBM) for array in small]
    messages = [(own, by) for own in range(owned) for by in out_order] + [(own, 0) for own in range(owned)]
    sent = {}
    shares = (messages[:1], messages[1:5], messages[5:])
    for step, part in enumerate(shares):
        extra = small if step == 0 else []
        source = pltpu.with_memory_space_constraint(sequence, pltpu.HBM) if step == 0 else sequence
        if step == 2:
            kernel, extra = functools.partial(deal_build_kernel, count, rows, lags, owned, group_w, part), list(map(held, small))
            added = [VMEM((owned, lags, rows, rows), BF16)] * 2 + [VMEM((owned, 8, group_w), F32)]
        else:
            kernel, added = functools.partial(deal_kernel, count, owned, group_w, part), [VMEM(a.shape, a.dtype) for a in extra]
        copied = pl.pallas_call(
            kernel,
            in_specs=[anywhere] + [vmem if step == 2 else anywhere] * len(extra),
            out_specs=[vmem] * (len(part) + len(added)),
            out_shape=[VMEM((rows, group_w), BF16) for _ in part] + added,
            scratch_shapes=[dma((len(part) + len(extra),))],
            compiler_params=params,
            name="deal",
        )(source, *extra)
        sent.update({(own, by): rotated(array, by) if by else array for (own, by), array in zip(part, copied)})
        small = copied[len(part) :] if step == 0 else small
    built = copied[len(part) :]
    back = []
    for own in range(owned):
        outs = pl.pallas_call(
            functools.partial(mix_kernel, count, lags, own, out_order, back_order),
            in_specs=[vmem] * (count + 3),
            out_specs=[vmem] * count,
            out_shape=[VMEM((rows, group_w), BF16)] * count,
            compiler_params=params,
            name="mix",
        )(*map(held, [*[sent[own, by] for by in (0, *out_order)], *built]))
        back.append([rotated(array, by) if by else array for by, array in zip((0, *back_order), outs)])
    gate = held(gate)
    out = []
    for own in range(owned):
        out = [
            pl.pallas_call(
                functools.partial(gate_kernel, count, owned, own, back_order),
                in_specs=[vmem] * (count + 1) + [anywhere] * len(out),
                out_specs=anywhere,
                out_shape=jax.ShapeDtypeStruct((rows, width), BF16),
                scratch_shapes=[VMEM((count, rows, group_w), BF16), dma((count,))],
                input_output_aliases={count + 1: 0} if out else {},
                compiler_params=params,
                name="gate",
            )(gate, *map(held, back[own]), *out)
        ]
    return out[0]


def build_blocks(kernel, rows):
    groups_dev, taps = kernel.shape
    padded = jnp.pad(kernel, ((0, 0), (rows, rows)))
    blocks = []
    for lag in range(taps // rows + 1):
        window = padded[:, lag * rows : lag * rows + 2 * rows][:, ::-1]
        tiled = jnp.tile(window, (1, rows))[:, : rows * (2 * rows - 1)]
        skewed = tiled.reshape(groups_dev, rows, 2 * rows - 1)
        blocks.append(skewed[:, :, rows - 1 : 2 * rows - 1])
    return blocks


def halos(sequence, gate, filters, lengths, gain, permutation):
    rows, width = sequence.shape
    groups_dev = filters.shape[0]
    group_w = permutation.shape[0]
    tap_ids = lax.broadcasted_iota(jnp.int32, filters.shape, 1)
    kernel = jnp.where(tap_ids < lengths[:, None] * rows, filters, 0.0).astype(BF16)
    blocks = build_blocks(kernel, rows)
    gain3 = gain.reshape(groups_dev, group_w)
    target_ids = lax.broadcasted_iota(jnp.int32, (group_w, group_w), 1)
    match = permutation[:, None] == target_ids
    gain_rc = jnp.sum(jnp.where(match[None], gain3[:, :, None], 0.0), axis=1)

    def scaled(block, gains):
        return (block.reshape(rows, groups_dev, group_w).astype(F32) * gains[None]).astype(BF16)

    ahead, behind = 0.0, 0.0
    for lag, matrix in enumerate(blocks):
        past = scaled(shifted(sequence, lag) if lag else sequence, gain3)
        later = scaled(shifted(sequence, -lag) if lag else sequence, gain_rc)
        ahead = ahead + jnp.einsum("gst,tgc->sgc", matrix, past, preferred_element_type=F32)
        behind = behind + jnp.einsum("gts,tgc->sgc", matrix, later, preferred_element_type=F32)
    gate3 = gate.reshape(rows, groups_dev, group_w).astype(F32)
    mixed = gate3 * (ahead + behind.astype(BF16).astype(F32))
    return mixed.astype(BF16).reshape(rows, width)


def body(*args):
    count = lax.axis_size("ctx")
    groups_dev = args[2].shape[0]
    if count <= 8 and groups_dev % count == 0:
        return dealt(*args)
    return halos(*args)


def solution(mesh):
    in_specs = (
        P(("groups", "ctx"), ("chan", "sub")),
        P(("groups", "ctx"), ("chan", "sub")),
        P(("chan", "sub"), None),
        P(("chan", "sub")),
        P(("chan", "sub")),
        P(),
    )
    out_specs = P(("groups", "ctx"), ("chan", "sub"))
    return jax.shard_map(body, mesh=mesh, in_specs=in_specs, out_specs=out_specs, check_vma=False)
```

```python
import functools

import jax
import jax.numpy as jnp
from jax import lax
from jax.experimental import pallas as pl
from jax.experimental.pallas import tpu as pltpu
from jax.sharding import PartitionSpec as P

F32, BF16 = jnp.float32, jnp.bfloat16
VMEM = pltpu.VMEM


def shifted(array, by):
    count = lax.axis_size("ctx")
    return lax.ppermute(array, "ctx", [(i, i + by) for i in range(count) if 0 <= i + by < count])


def rotated(array, by):
    count = lax.axis_size("ctx")
    return lax.ppermute(array, "ctx", [(i, (i + by) % count) for i in range(count)])


def returned(array, bys):
    count, cores = lax.axis_size("ctx"), lax.axis_size("sub")
    pairs = [(i * cores + c, (i + bys[c % 2]) % count * cores + c) for c in range(cores) for i in range(count)]
    return lax.ppermute(array, ("ctx", "sub"), pairs)


def held(array):
    return pltpu.with_memory_space_constraint(array, VMEM)


def rounds(count):
    if count == 4:
        return (2, 1, 3), (((1, 2, 3), (1, 2, 3)), ((1, 2, 3), (2, 1, 3)))
    plain = tuple(range(1, count))
    return plain, ((plain, plain),) * 8


def lanes(by, own, count, owned, group_w):
    block = lax.rem(lax.axis_index("ctx") + by, count)
    return pl.ds(pl.multiple_of((block * owned + own) * group_w, group_w), group_w)


def build_kernel(rows, lags, owned, owns, filters_ref, lengths_ref, gain_ref, perm_ref, fwd_ref, bwd_ref, gains_ref):
    first = lax.axis_index("ctx") * owned
    group_w = perm_ref.shape[1]
    taps = filters_ref.shape[1]
    span = lags * rows
    target = lax.broadcasted_iota(jnp.int32, (group_w, group_w), 0)
    match = perm_ref[...] == target
    group_ids = lax.broadcasted_iota(jnp.int32, lengths_ref.shape, 1)
    tap_ids = lax.broadcasted_iota(jnp.int32, (1, taps), 1)
    for at, own in enumerate(owns):
        group = first + own
        length = jnp.sum(jnp.where(group_ids == group, lengths_ref[...], 0), axis=1, keepdims=True)
        taps_row = jnp.where(tap_ids < length * rows, filters_ref[pl.ds(group, 1), :], 0.0)
        taps_row = jnp.concatenate([taps_row, jnp.zeros((1, span - taps), F32)], axis=1)
        strip = pltpu.roll(jnp.broadcast_to(taps_row, (rows, span)), 0, 1, stride=1, stride_axis=0)
        for lag in range(lags):
            block = strip[:, lag * rows : (lag + 1) * rows]
            bwd_ref[at, lag] = block.astype(BF16)
            fwd_ref[at, lag] = block.T.astype(BF16)
        gain_row = gain_ref[pl.ds(group, 1), :]
        spread = jnp.where(match, gain_row, 0.0)
        gains_ref[at, 0:1, :] = gain_row
        gains_ref[at, 1:2, :] = jnp.sum(spread.T, axis=0, keepdims=True)


def deal_kernel(count, owned, group_w, messages, x_ref, *refs):
    sems = refs[-1]
    small = (len(refs) - 1 - len(messages)) // 2
    outs = refs[small:-1]
    sources = [x_ref.at[:, lanes(by, own, count, owned, group_w)] for own, by in messages] + list(refs[:small])
    copies = [pltpu.make_async_copy(source, outs[i], sems.at[i]) for i, source in enumerate(sources)]
    for copy in copies:
        copy.start()
    for copy in copies:
        copy.wait()


def deal_build_kernel(count, rows, lags, owned, group_w, messages, x_ref, *refs):
    small, outs, built, sems = refs[:4], refs[4 : 4 + len(messages)], refs[4 + len(messages) : -1], refs[-1]
    copies = [
        pltpu.make_async_copy(x_ref.at[:, lanes(by, own, count, owned, group_w)], outs[i], sems.at[i])
        for i, (own, by) in enumerate(messages)
    ]
    for copy in copies:
        copy.start()
    build_kernel(rows, lags, owned, tuple(range(owned)), *small, *built)
    for copy in copies:
        copy.wait()


def mix_kernel(count, lags, own, out_order, back_order, *refs):
    core = lax.rem(lax.axis_index("sub"), 2)
    same = back_order[0] == back_order[1]
    for me in range(count):
        here = lax.axis_index("ctx") == me
        for at in range(1 if same else 2):
            body = functools.partial(mix_at, me, count, lags, own, out_order, back_order[at], *refs)
            pl.when(here if same else here & (core == at))(body)


def mix_at(me, count, lags, own, out_order, back_order, *refs):
    blocks, (fwd_ref, bwd_ref, gains_ref), outs = refs[:count], refs[count : count + 3], refs[count + 3 :]
    group_w = gains_ref.shape[2]
    inputs = {(me - by) % count: block for block, by in zip(blocks, (0, *out_order))}
    sums = {(me + by) % count: out for out, by in zip(outs, (0, *back_order))}
    values = [inputs[i][...].astype(F32) for i in range(count)]
    gated = jnp.concatenate([(value * gains_ref[own, 0:1, :]).astype(BF16) for value in values], axis=1)
    flipped = jnp.concatenate([(value * gains_ref[own, 1:2, :]).astype(BF16) for value in values], axis=1)
    ahead = [None] * count
    behind = [None] * count

    def add(total, at, value):
        total[at] = value if total[at] is None else total[at] + value

    for lag in range(min(lags, count)):
        kept = (count - lag) * group_w
        up = jnp.dot(fwd_ref[own, lag], gated[:, :kept], preferred_element_type=F32)
        down = jnp.dot(bwd_ref[own, lag], flipped[:, count * group_w - kept :], preferred_element_type=F32)
        for i in range(count - lag):
            piece = slice(i * group_w, (i + 1) * group_w)
            add(ahead, i + lag, up[:, piece])
            add(behind, i, down[:, piece])
    for i in range(count):
        sums[i][...] = (ahead[i] + behind[i].astype(BF16).astype(F32)).astype(BF16)


def gate_kernel(count, owned, own, back_order, gate_ref, *refs):
    blocks, out_ref, (pieces, sems) = refs[:count], refs[-3], refs[-2:]
    group_w = blocks[0].shape[1]
    copies = []
    core = lax.rem(lax.axis_index("sub"), 2)
    for i, (first, second) in enumerate(zip((0, *back_order[0]), (0, *back_order[1]))):
        by = first if first == second else jnp.where(core == 0, first, second)
        place = lanes(count - by, own, count, owned, group_w)
        pieces[i] = (gate_ref[:, place].astype(F32) * blocks[i][...].astype(F32)).astype(BF16)
        copies.append(pltpu.make_async_copy(pieces.at[i], out_ref.at[:, place], sems.at[i]))
        copies[i].start()
    for copy in copies:
        copy.wait()


def dealt(sequence, gate, filters, lengths, gain, permutation):
    rows, width = sequence.shape
    count = lax.axis_size("ctx")
    groups_dev, taps = filters.shape
    group_w = permutation.shape[0]
    owned = groups_dev // count
    lags = taps // rows + 1
    out_order, back_order = rounds(count)
    vmem, anywhere = pl.BlockSpec(memory_space=VMEM), pl.BlockSpec(memory_space=pl.ANY)
    params = pltpu.CompilerParams(vmem_limit_bytes=24 << 20)
    dma = pltpu.SemaphoreType.DMA

    small = [
        filters,
        lengths.reshape(1, groups_dev),
        gain.reshape(groups_dev, group_w),
        permutation.reshape(1, group_w),
    ]
    small = [pltpu.with_memory_space_constraint(array, pltpu.HBM) for array in small]
    messages = [(own, by) for own in range(owned) for by in out_order] + [(own, 0) for own in range(owned)]
    sent = {}
    shares = (messages[:1], messages[1:5], messages[5:])
    for step, part in enumerate(shares):
        extra = small if step == 0 else []
        source = pltpu.with_memory_space_constraint(sequence, pltpu.HBM) if step == 0 else sequence
        if step == 2:
            kernel, extra = functools.partial(deal_build_kernel, count, rows, lags, owned, group_w, part), list(map(held, small))
            added = [VMEM((owned, lags, rows, rows), BF16)] * 2 + [VMEM((owned, 8, group_w), F32)]
        else:
            kernel, added = functools.partial(deal_kernel, count, owned, group_w, part), [VMEM(a.shape, a.dtype) for a in extra]
        copied = pl.pallas_call(
            kernel,
            in_specs=[anywhere] + [vmem if step == 2 else anywhere] * len(extra),
            out_specs=[vmem] * (len(part) + len(added)),
            out_shape=[VMEM((rows, group_w), BF16) for _ in part] + added,
            scratch_shapes=[dma((len(part) + len(extra),))],
            compiler_params=params,
            name="deal",
        )(source, *extra)
        sent.update({(own, by): rotated(array, by) if by else array for (own, by), array in zip(part, copied)})
        small = copied[len(part) :] if step == 0 else small
    built = copied[len(part) :]
    back = []
    for own in range(owned):
        outs = pl.pallas_call(
            functools.partial(mix_kernel, count, lags, own, out_order, back_order[own]),
            in_specs=[vmem] * (count + 3),
            out_specs=[vmem] * count,
            out_shape=[VMEM((rows, group_w), BF16)] * count,
            compiler_params=params,
            name="mix",
        )(*map(held, [*[sent[own, by] for by in (0, *out_order)], *built]))
        back.append([outs[0]] + [returned(array, bys) for bys, array in zip(zip(*back_order[own]), outs[1:])])
    gate = held(gate)
    out = []
    for own in range(owned):
        out = [
            pl.pallas_call(
                functools.partial(gate_kernel, count, owned, own, back_order[own]),
                in_specs=[vmem] * (count + 1) + [anywhere] * len(out),
                out_specs=anywhere,
                out_shape=jax.ShapeDtypeStruct((rows, width), BF16),
                scratch_shapes=[VMEM((count, rows, group_w), BF16), dma((count,))],
                input_output_aliases={count + 1: 0} if out else {},
                compiler_params=params,
                name="gate",
            )(gate, *map(held, back[own]), *out)
        ]
    return out[0]


def build_blocks(kernel, rows):
    groups_dev, taps = kernel.shape
    padded = jnp.pad(kernel, ((0, 0), (rows, rows)))
    blocks = []
    for lag in range(taps // rows + 1):
        window = padded[:, lag * rows : lag * rows + 2 * rows][:, ::-1]
        tiled = jnp.tile(window, (1, rows))[:, : rows * (2 * rows - 1)]
        skewed = tiled.reshape(groups_dev, rows, 2 * rows - 1)
        blocks.append(skewed[:, :, rows - 1 : 2 * rows - 1])
    return blocks


def halos(sequence, gate, filters, lengths, gain, permutation):
    rows, width = sequence.shape
    groups_dev = filters.shape[0]
    group_w = permutation.shape[0]
    tap_ids = lax.broadcasted_iota(jnp.int32, filters.shape, 1)
    kernel = jnp.where(tap_ids < lengths[:, None] * rows, filters, 0.0).astype(BF16)
    blocks = build_blocks(kernel, rows)
    gain3 = gain.reshape(groups_dev, group_w)
    target_ids = lax.broadcasted_iota(jnp.int32, (group_w, group_w), 1)
    match = permutation[:, None] == target_ids
    gain_rc = jnp.sum(jnp.where(match[None], gain3[:, :, None], 0.0), axis=1)

    def scaled(block, gains):
        return (block.reshape(rows, groups_dev, group_w).astype(F32) * gains[None]).astype(BF16)

    ahead, behind = 0.0, 0.0
    for lag, matrix in enumerate(blocks):
        past = scaled(shifted(sequence, lag) if lag else sequence, gain3)
        later = scaled(shifted(sequence, -lag) if lag else sequence, gain_rc)
        ahead = ahead + jnp.einsum("gst,tgc->sgc", matrix, past, preferred_element_type=F32)
        behind = behind + jnp.einsum("gts,tgc->sgc", matrix, later, preferred_element_type=F32)
    gate3 = gate.reshape(rows, groups_dev, group_w).astype(F32)
    mixed = gate3 * (ahead + behind.astype(BF16).astype(F32))
    return mixed.astype(BF16).reshape(rows, width)


def body(*args):
    count = lax.axis_size("ctx")
    groups_dev = args[2].shape[0]
    if count <= 8 and groups_dev % count == 0:
        return dealt(*args)
    return halos(*args)


def solution(mesh):
    in_specs = (
        P(("groups", "ctx"), ("chan", "sub")),
        P(("groups", "ctx"), ("chan", "sub")),
        P(("chan", "sub"), None),
        P(("chan", "sub")),
        P(("chan", "sub")),
        P(),
    )
    out_specs = P(("groups", "ctx"), ("chan", "sub"))
    return jax.shard_map(body, mesh=mesh, in_specs=in_specs, out_specs=out_specs, check_vma=False)
```

```python
import functools

import jax
import jax.numpy as jnp
from jax import lax
from jax.experimental import pallas as pl
from jax.experimental.pallas import tpu as pltpu
from jax.sharding import PartitionSpec as P

F32, BF16 = jnp.float32, jnp.bfloat16
VMEM = pltpu.VMEM


def shifted(array, by):
    count = lax.axis_size("ctx")
    return lax.ppermute(array, "ctx", [(i, i + by) for i in range(count) if 0 <= i + by < count])


def rotated(array, by):
    count = lax.axis_size("ctx")
    return lax.ppermute(array, "ctx", [(i, (i + by) % count) for i in range(count)])


def held(array):
    return pltpu.with_memory_space_constraint(array, VMEM)


def rounds(count):
    if count == 4:
        return (2, 1, 3), (1, 2, 3)
    return (tuple(range(1, count)),) * 2


def lanes(by, own, count, owned, group_w):
    block = lax.rem(lax.axis_index("ctx") + by, count)
    return pl.ds(pl.multiple_of((block * owned + own) * group_w, group_w), group_w)


def build_kernel(rows, lags, owned, owns, filters_ref, lengths_ref, gain_ref, perm_ref, fwd_ref, bwd_ref, gains_ref):
    first = lax.axis_index("ctx") * owned
    group_w = perm_ref.shape[1]
    taps = filters_ref.shape[1]
    span = lags * rows
    target = lax.broadcasted_iota(jnp.int32, (group_w, group_w), 0)
    match = perm_ref[...] == target
    group_ids = lax.broadcasted_iota(jnp.int32, lengths_ref.shape, 1)
    tap_ids = lax.broadcasted_iota(jnp.int32, (1, taps), 1)
    for at, own in enumerate(owns):
        group = first + own
        length = jnp.sum(jnp.where(group_ids == group, lengths_ref[...], 0), axis=1, keepdims=True)
        taps_row = jnp.where(tap_ids < length * rows, filters_ref[pl.ds(group, 1), :], 0.0)
        taps_row = jnp.concatenate([taps_row, jnp.zeros((1, span - taps), F32)], axis=1)
        strip = pltpu.roll(jnp.broadcast_to(taps_row, (rows, span)), 0, 1, stride=1, stride_axis=0)
        for lag in range(lags):
            block = strip[:, lag * rows : (lag + 1) * rows]
            bwd_ref[at, lag] = block.astype(BF16)
            fwd_ref[at, lag] = block.T.astype(BF16)
        gain_row = gain_ref[pl.ds(group, 1), :]
        spread = jnp.where(match, gain_row, 0.0)
        gains_ref[at, 0:1, :] = gain_row
        gains_ref[at, 1:2, :] = jnp.sum(spread.T, axis=0, keepdims=True)


def deal_kernel(count, owned, group_w, messages, x_ref, *refs):
    sems = refs[-1]
    small = (len(refs) - 1 - len(messages)) // 2
    outs = refs[small:-1]
    sources = [x_ref.at[:, lanes(by, own, count, owned, group_w)] for own, by in messages] + list(refs[:small])
    copies = [pltpu.make_async_copy(source, outs[i], sems.at[i]) for i, source in enumerate(sources)]
    for copy in copies:
        copy.start()
    for copy in copies:
        copy.wait()


def deal_build_kernel(count, rows, lags, owned, group_w, messages, x_ref, *refs):
    small, outs, built, sems = refs[:4], refs[4 : 4 + len(messages)], refs[4 + len(messages) : -1], refs[-1]
    copies = [
        pltpu.make_async_copy(x_ref.at[:, lanes(by, own, count, owned, group_w)], outs[i], sems.at[i])
        for i, (own, by) in enumerate(messages)
    ]
    for copy in copies:
        copy.start()
    build_kernel(rows, lags, owned, tuple(range(owned)), *small, *built)
    for copy in copies:
        copy.wait()


def mix_kernel(count, lags, own, out_order, back_order, *refs):
    for me in range(count):
        body = functools.partial(mix_at, me, count, lags, own, out_order, back_order, *refs)
        pl.when(lax.axis_index("ctx") == me)(body)


def mix_at(me, count, lags, own, out_order, back_order, *refs):
    blocks, (fwd_ref, bwd_ref, gains_ref), outs = refs[:count], refs[count : count + 3], refs[count + 3 :]
    group_w = gains_ref.shape[2]
    inputs = {(me - by) % count: block for block, by in zip(blocks, (0, *out_order))}
    sums = {(me + by) % count: out for out, by in zip(outs, (0, *back_order))}
    values = [inputs[i][...].astype(F32) for i in range(count)]
    gated = jnp.concatenate([(value * gains_ref[own, 0:1, :]).astype(BF16) for value in values], axis=1)
    flipped = jnp.concatenate([(value * gains_ref[own, 1:2, :]).astype(BF16) for value in values], axis=1)
    ahead = [None] * count
    behind = [None] * count

    def add(total, at, value):
        total[at] = value if total[at] is None else total[at] + value

    for lag in range(min(lags, count)):
        kept = (count - lag) * group_w
        up = jnp.dot(fwd_ref[own, lag], gated[:, :kept], preferred_element_type=F32)
        down = jnp.dot(bwd_ref[own, lag], flipped[:, count * group_w - kept :], preferred_element_type=F32)
        for i in range(count - lag):
            piece = slice(i * group_w, (i + 1) * group_w)
            add(ahead, i + lag, up[:, piece])
            add(behind, i, down[:, piece])
    for i in range(count):
        sums[i][...] = (ahead[i] + behind[i].astype(BF16).astype(F32)).astype(BF16)


def gate_kernel(count, owned, own, back_order, gate_ref, *refs):
    blocks, out_ref, (pieces, sems) = refs[:count], refs[-3], refs[-2:]
    group_w = blocks[0].shape[1]
    copies = []
    for i, by in enumerate((0, *back_order)):
        place = lanes(count - by, own, count, owned, group_w)
        pieces[i] = gate_ref[:, place] * blocks[i][...]
        copies.append(pltpu.make_async_copy(pieces.at[i], out_ref.at[:, place], sems.at[i]))
        copies[i].start()
    for copy in copies:
        copy.wait()


def dealt(sequence, gate, filters, lengths, gain, permutation):
    rows, width = sequence.shape
    count = lax.axis_size("ctx")
    groups_dev, taps = filters.shape
    group_w = permutation.shape[0]
    owned = groups_dev // count
    lags = taps // rows + 1
    out_order, back_order = rounds(count)
    vmem, anywhere = pl.BlockSpec(memory_space=VMEM), pl.BlockSpec(memory_space=pl.ANY)
    params = pltpu.CompilerParams(vmem_limit_bytes=24 << 20)
    dma = pltpu.SemaphoreType.DMA

    small = [
        filters,
        lengths.reshape(1, groups_dev),
        gain.reshape(groups_dev, group_w),
        permutation.reshape(1, group_w),
    ]
    small = [pltpu.with_memory_space_constraint(array, pltpu.HBM) for array in small]
    messages = [(own, by) for own in range(owned) for by in out_order] + [(own, 0) for own in range(owned)]
    sent = {}
    shares = (messages[:1], messages[1:5], messages[5:])
    for step, part in enumerate(shares):
        extra = small if step == 0 else []
        source = pltpu.with_memory_space_constraint(sequence, pltpu.HBM) if step == 0 else sequence
        if step == 2:
            kernel, extra = functools.partial(deal_build_kernel, count, rows, lags, owned, group_w, part), list(map(held, small))
            added = [VMEM((owned, lags, rows, rows), BF16)] * 2 + [VMEM((owned, 8, group_w), F32)]
        else:
            kernel, added = functools.partial(deal_kernel, count, owned, group_w, part), [VMEM(a.shape, a.dtype) for a in extra]
        copied = pl.pallas_call(
            kernel,
            in_specs=[anywhere] + [vmem if step == 2 else anywhere] * len(extra),
            out_specs=[vmem] * (len(part) + len(added)),
            out_shape=[VMEM((rows, group_w), BF16) for _ in part] + added,
            scratch_shapes=[dma((len(part) + len(extra),))],
            compiler_params=params,
            name="deal",
        )(source, *extra)
        sent.update({(own, by): rotated(array, by) if by else array for (own, by), array in zip(part, copied)})
        small = copied[len(part) :] if step == 0 else small
    built = copied[len(part) :]
    back = []
    for own in range(owned):
        outs = pl.pallas_call(
            functools.partial(mix_kernel, count, lags, own, out_order, back_order),
            in_specs=[vmem] * (count + 3),
            out_specs=[vmem] * count,
            out_shape=[VMEM((rows, group_w), BF16)] * count,
            compiler_params=params,
            name="mix",
        )(*map(held, [*[sent[own, by] for by in (0, *out_order)], *built]))
        back.append([rotated(array, by) if by else array for by, array in zip((0, *back_order), outs)])
    gate = held(gate)
    out = []
    for own in range(owned):
        out = [
            pl.pallas_call(
                functools.partial(gate_kernel, count, owned, own, back_order),
                in_specs=[vmem] * (count + 1) + [anywhere] * len(out),
                out_specs=anywhere,
                out_shape=jax.ShapeDtypeStruct((rows, width), BF16),
                scratch_shapes=[VMEM((count, rows, group_w), BF16), dma((count,))],
                input_output_aliases={count + 1: 0} if out else {},
                compiler_params=params,
                name="gate",
            )(gate, *map(held, back[own]), *out)
        ]
    return out[0]


def build_blocks(kernel, rows):
    groups_dev, taps = kernel.shape
    padded = jnp.pad(kernel, ((0, 0), (rows, rows)))
    blocks = []
    for lag in range(taps // rows + 1):
        window = padded[:, lag * rows : lag * rows + 2 * rows][:, ::-1]
        tiled = jnp.tile(window, (1, rows))[:, : rows * (2 * rows - 1)]
        skewed = tiled.reshape(groups_dev, rows, 2 * rows - 1)
        blocks.append(skewed[:, :, rows - 1 : 2 * rows - 1])
    return blocks


def halos(sequence, gate, filters, lengths, gain, permutation):
    rows, width = sequence.shape
    groups_dev = filters.shape[0]
    group_w = permutation.shape[0]
    tap_ids = lax.broadcasted_iota(jnp.int32, filters.shape, 1)
    kernel = jnp.where(tap_ids < lengths[:, None] * rows, filters, 0.0).astype(BF16)
    blocks = build_blocks(kernel, rows)
    gain3 = gain.reshape(groups_dev, group_w)
    target_ids = lax.broadcasted_iota(jnp.int32, (group_w, group_w), 1)
    match = permutation[:, None] == target_ids
    gain_rc = jnp.sum(jnp.where(match[None], gain3[:, :, None], 0.0), axis=1)

    def scaled(block, gains):
        return (block.reshape(rows, groups_dev, group_w).astype(F32) * gains[None]).astype(BF16)

    ahead, behind = 0.0, 0.0
    for lag, matrix in enumerate(blocks):
        past = scaled(shifted(sequence, lag) if lag else sequence, gain3)
        later = scaled(shifted(sequence, -lag) if lag else sequence, gain_rc)
        ahead = ahead + jnp.einsum("gst,tgc->sgc", matrix, past, preferred_element_type=F32)
        behind = behind + jnp.einsum("gts,tgc->sgc", matrix, later, preferred_element_type=F32)
    gate3 = gate.reshape(rows, groups_dev, group_w).astype(F32)
    mixed = gate3 * (ahead + behind.astype(BF16).astype(F32))
    return mixed.astype(BF16).reshape(rows, width)


def body(*args):
    count = lax.axis_size("ctx")
    groups_dev = args[2].shape[0]
    if count <= 8 and groups_dev % count == 0:
        return dealt(*args)
    return halos(*args)


def solution(mesh):
    in_specs = (
        P(("groups", "ctx"), ("chan", "sub")),
        P(("groups", "ctx"), ("chan", "sub")),
        P(("chan", "sub"), None),
        P(("chan", "sub")),
        P(("chan", "sub")),
        P(),
    )
    out_specs = P(("groups", "ctx"), ("chan", "sub"))
    return jax.shard_map(body, mesh=mesh, in_specs=in_specs, out_specs=out_specs, check_vma=False)
```

```python
import functools

import jax
import jax.numpy as jnp
from jax import lax
from jax.experimental import pallas as pl
from jax.experimental.pallas import tpu as pltpu
from jax.sharding import PartitionSpec as P

F32, BF16 = jnp.float32, jnp.bfloat16
VMEM = pltpu.VMEM


def shifted(array, by):
    count = lax.axis_size("ctx")
    return lax.ppermute(array, "ctx", [(i, i + by) for i in range(count) if 0 <= i + by < count])


def rotated(array, by):
    count = lax.axis_size("ctx")
    return lax.ppermute(array, "ctx", [(i, (i + by) % count) for i in range(count)])


def returned(array, bys):
    count, cores = lax.axis_size("ctx"), lax.axis_size("sub")
    pairs = [(i * cores + c, (i + bys[c % 2]) % count * cores + c) for c in range(cores) for i in range(count)]
    return lax.ppermute(array, ("ctx", "sub"), pairs)


def held(array):
    return pltpu.with_memory_space_constraint(array, VMEM)


def rounds(count):
    if count == 4:
        return (2, 1, 3), (((1, 2, 3), (1, 2, 3)), ((2, 1, 3), (2, 1, 3)))
    plain = tuple(range(1, count))
    return plain, ((plain, plain),) * 8


def lanes(by, own, count, owned, group_w):
    block = lax.rem(lax.axis_index("ctx") + by, count)
    return pl.ds(pl.multiple_of((block * owned + own) * group_w, group_w), group_w)


def build_kernel(rows, lags, owned, owns, filters_ref, lengths_ref, gain_ref, perm_ref, fwd_ref, bwd_ref, gains_ref):
    first = lax.axis_index("ctx") * owned
    group_w = perm_ref.shape[1]
    taps = filters_ref.shape[1]
    span = lags * rows
    target = lax.broadcasted_iota(jnp.int32, (group_w, group_w), 0)
    match = perm_ref[...] == target
    group_ids = lax.broadcasted_iota(jnp.int32, lengths_ref.shape, 1)
    tap_ids = lax.broadcasted_iota(jnp.int32, (1, taps), 1)
    for at, own in enumerate(owns):
        group = first + own
        length = jnp.sum(jnp.where(group_ids == group, lengths_ref[...], 0), axis=1, keepdims=True)
        taps_row = jnp.where(tap_ids < length * rows, filters_ref[pl.ds(group, 1), :], 0.0)
        taps_row = jnp.concatenate([taps_row, jnp.zeros((1, span - taps), F32)], axis=1)
        strip = pltpu.roll(jnp.broadcast_to(taps_row, (rows, span)), 0, 1, stride=1, stride_axis=0)
        for lag in range(lags):
            block = strip[:, lag * rows : (lag + 1) * rows]
            bwd_ref[at, lag] = block.astype(BF16)
            fwd_ref[at, lag] = block.T.astype(BF16)
        gain_row = gain_ref[pl.ds(group, 1), :]
        spread = jnp.where(match, gain_row, 0.0)
        gains_ref[at, 0:1, :] = gain_row
        gains_ref[at, 1:2, :] = jnp.sum(spread.T, axis=0, keepdims=True)


def deal_kernel(count, owned, group_w, messages, x_ref, *refs):
    sems = refs[-1]
    small = (len(refs) - 1 - len(messages)) // 2
    outs = refs[small:-1]
    sources = [x_ref.at[:, lanes(by, own, count, owned, group_w)] for own, by in messages] + list(refs[:small])
    copies = [pltpu.make_async_copy(source, outs[i], sems.at[i]) for i, source in enumerate(sources)]
    for copy in copies:
        copy.start()
    for copy in copies:
        copy.wait()


def deal_build_kernel(count, rows, lags, owned, group_w, messages, x_ref, *refs):
    small, outs, built, sems = refs[:4], refs[4 : 4 + len(messages)], refs[4 + len(messages) : -1], refs[-1]
    copies = [
        pltpu.make_async_copy(x_ref.at[:, lanes(by, own, count, owned, group_w)], outs[i], sems.at[i])
        for i, (own, by) in enumerate(messages)
    ]
    for copy in copies:
        copy.start()
    build_kernel(rows, lags, owned, tuple(range(owned)), *small, *built)
    for copy in copies:
        copy.wait()


def mix_kernel(count, lags, own, out_order, back_order, *refs):
    core = lax.rem(lax.axis_index("sub"), 2)
    same = back_order[0] == back_order[1]
    for me in range(count):
        here = lax.axis_index("ctx") == me
        for at in range(1 if same else 2):
            body = functools.partial(mix_at, me, count, lags, own, out_order, back_order[at], *refs)
            pl.when(here if same else here & (core == at))(body)


def mix_at(me, count, lags, own, out_order, back_order, *refs):
    blocks, (fwd_ref, bwd_ref, gains_ref), outs = refs[:count], refs[count : count + 3], refs[count + 3 :]
    group_w = gains_ref.shape[2]
    inputs = {(me - by) % count: block for block, by in zip(blocks, (0, *out_order))}
    sums = {(me + by) % count: out for out, by in zip(outs, (0, *back_order))}
    values = [inputs[i][...].astype(F32) for i in range(count)]
    gated = jnp.concatenate([(value * gains_ref[own, 0:1, :]).astype(BF16) for value in values], axis=1)
    flipped = jnp.concatenate([(value * gains_ref[own, 1:2, :]).astype(BF16) for value in values], axis=1)
    ahead = [None] * count
    behind = [None] * count

    def add(total, at, value):
        total[at] = value if total[at] is None else total[at] + value

    for lag in range(min(lags, count)):
        kept = (count - lag) * group_w
        up = jnp.dot(fwd_ref[own, lag], gated[:, :kept], preferred_element_type=F32)
        down = jnp.dot(bwd_ref[own, lag], flipped[:, count * group_w - kept :], preferred_element_type=F32)
        for i in range(count - lag):
            piece = slice(i * group_w, (i + 1) * group_w)
            add(ahead, i + lag, up[:, piece])
            add(behind, i, down[:, piece])
    for i in range(count):
        sums[i][...] = (ahead[i] + behind[i].astype(BF16).astype(F32)).astype(BF16)


def gate_kernel(count, owned, own, back_order, gate_ref, *refs):
    blocks, out_ref, (pieces, sems) = refs[:count], refs[-3], refs[-2:]
    group_w = blocks[0].shape[1]
    copies = []
    core = lax.rem(lax.axis_index("sub"), 2)
    for i, (first, second) in enumerate(zip((0, *back_order[0]), (0, *back_order[1]))):
        by = first if first == second else jnp.where(core == 0, first, second)
        place = lanes(count - by, own, count, owned, group_w)
        pieces[i] = (gate_ref[:, place].astype(F32) * blocks[i][...].astype(F32)).astype(BF16)
        copies.append(pltpu.make_async_copy(pieces.at[i], out_ref.at[:, place], sems.at[i]))
        copies[i].start()
    for copy in copies:
        copy.wait()


def dealt(sequence, gate, filters, lengths, gain, permutation):
    rows, width = sequence.shape
    count = lax.axis_size("ctx")
    groups_dev, taps = filters.shape
    group_w = permutation.shape[0]
    owned = groups_dev // count
    lags = taps // rows + 1
    out_order, back_order = rounds(count)
    vmem, anywhere = pl.BlockSpec(memory_space=VMEM), pl.BlockSpec(memory_space=pl.ANY)
    params = pltpu.CompilerParams(vmem_limit_bytes=24 << 20)
    dma = pltpu.SemaphoreType.DMA

    small = [
        filters,
        lengths.reshape(1, groups_dev),
        gain.reshape(groups_dev, group_w),
        permutation.reshape(1, group_w),
    ]
    small = [pltpu.with_memory_space_constraint(array, pltpu.HBM) for array in small]
    messages = [(own, by) for own in range(owned) for by in out_order] + [(own, 0) for own in range(owned)]
    sent = {}
    shares = (messages[:1], messages[1:5], messages[5:])
    for step, part in enumerate(shares):
        extra = small if step == 0 else []
        source = pltpu.with_memory_space_constraint(sequence, pltpu.HBM) if step == 0 else sequence
        if step == 2:
            kernel, extra = functools.partial(deal_build_kernel, count, rows, lags, owned, group_w, part), list(map(held, small))
            added = [VMEM((owned, lags, rows, rows), BF16)] * 2 + [VMEM((owned, 8, group_w), F32)]
        else:
            kernel, added = functools.partial(deal_kernel, count, owned, group_w, part), [VMEM(a.shape, a.dtype) for a in extra]
        copied = pl.pallas_call(
            kernel,
            in_specs=[anywhere] + [vmem if step == 2 else anywhere] * len(extra),
            out_specs=[vmem] * (len(part) + len(added)),
            out_shape=[VMEM((rows, group_w), BF16) for _ in part] + added,
            scratch_shapes=[dma((len(part) + len(extra),))],
            compiler_params=params,
            name="deal",
        )(source, *extra)
        sent.update({(own, by): rotated(array, by) if by else array for (own, by), array in zip(part, copied)})
        small = copied[len(part) :] if step == 0 else small
    built = copied[len(part) :]
    back = []
    for own in range(owned):
        outs = pl.pallas_call(
            functools.partial(mix_kernel, count, lags, own, out_order, back_order[own]),
            in_specs=[vmem] * (count + 3),
            out_specs=[vmem] * count,
            out_shape=[VMEM((rows, group_w), BF16)] * count,
            compiler_params=params,
            name="mix",
        )(*map(held, [*[sent[own, by] for by in (0, *out_order)], *built]))
        back.append([outs[0]] + [returned(array, bys) for bys, array in zip(zip(*back_order[own]), outs[1:])])
    gate = held(gate)
    out = []
    for own in range(owned):
        out = [
            pl.pallas_call(
                functools.partial(gate_kernel, count, owned, own, back_order[own]),
                in_specs=[vmem] * (count + 1) + [anywhere] * len(out),
                out_specs=anywhere,
                out_shape=jax.ShapeDtypeStruct((rows, width), BF16),
                scratch_shapes=[VMEM((count, rows, group_w), BF16), dma((count,))],
                input_output_aliases={count + 1: 0} if out else {},
                compiler_params=params,
                name="gate",
            )(gate, *map(held, back[own]), *out)
        ]
    return out[0]


def build_blocks(kernel, rows):
    groups_dev, taps = kernel.shape
    padded = jnp.pad(kernel, ((0, 0), (rows, rows)))
    blocks = []
    for lag in range(taps // rows + 1):
        window = padded[:, lag * rows : lag * rows + 2 * rows][:, ::-1]
        tiled = jnp.tile(window, (1, rows))[:, : rows * (2 * rows - 1)]
        skewed = tiled.reshape(groups_dev, rows, 2 * rows - 1)
        blocks.append(skewed[:, :, rows - 1 : 2 * rows - 1])
    return blocks


def halos(sequence, gate, filters, lengths, gain, permutation):
    rows, width = sequence.shape
    groups_dev = filters.shape[0]
    group_w = permutation.shape[0]
    tap_ids = lax.broadcasted_iota(jnp.int32, filters.shape, 1)
    kernel = jnp.where(tap_ids < lengths[:, None] * rows, filters, 0.0).astype(BF16)
    blocks = build_blocks(kernel, rows)
    gain3 = gain.reshape(groups_dev, group_w)
    target_ids = lax.broadcasted_iota(jnp.int32, (group_w, group_w), 1)
    match = permutation[:, None] == target_ids
    gain_rc = jnp.sum(jnp.where(match[None], gain3[:, :, None], 0.0), axis=1)

    def scaled(block, gains):
        return (block.reshape(rows, groups_dev, group_w).astype(F32) * gains[None]).astype(BF16)

    ahead, behind = 0.0, 0.0
    for lag, matrix in enumerate(blocks):
        past = scaled(shifted(sequence, lag) if lag else sequence, gain3)
        later = scaled(shifted(sequence, -lag) if lag else sequence, gain_rc)
        ahead = ahead + jnp.einsum("gst,tgc->sgc", matrix, past, preferred_element_type=F32)
        behind = behind + jnp.einsum("gts,tgc->sgc", matrix, later, preferred_element_type=F32)
    gate3 = gate.reshape(rows, groups_dev, group_w).astype(F32)
    mixed = gate3 * (ahead + behind.astype(BF16).astype(F32))
    return mixed.astype(BF16).reshape(rows, width)


def body(*args):
    count = lax.axis_size("ctx")
    groups_dev = args[2].shape[0]
    if count <= 8 and groups_dev % count == 0:
        return dealt(*args)
    return halos(*args)


def solution(mesh):
    in_specs = (
        P(("groups", "ctx"), ("chan", "sub")),
        P(("groups", "ctx"), ("chan", "sub")),
        P(("chan", "sub"), None),
        P(("chan", "sub")),
        P(("chan", "sub")),
        P(),
    )
    out_specs = P(("groups", "ctx"), ("chan", "sub"))
    return jax.shard_map(body, mesh=mesh, in_specs=in_specs, out_specs=out_specs, check_vma=False)
```
